32 devices in a mesh: expert: 4 (over x, core), shard: 8 (over z, y).
Axes of the slice: x: 2, y: 2, z: 4, core: 2. Of those that a mesh axis runs over, the one named last changes fastest.
Arguments:
- tokens_in: bfloat16 [1024, 4096], P(('expert', 'shard')), may hold values from -6 to 6
- out_grad: bfloat16 [1024, 2, 8192], P(('expert', 'shard')), may hold values from -6 to 6
- expert_ids: int32 [1024, 2], P(('expert', 'shard')), may hold values from 0 to 3, all different within a row; in each aligned block of 32 rows (0 to 31, 32 to 63, ...) at most 20 rows name the same one
- d_levels: int32 [4, 16], P('expert'), may hold values from 0 to 7
- f_levels: int32 [4, 32], P('expert', 'shard'), may hold values from 0 to 7
Outputs:
- ascent: bfloat16 [4, 4096, 8192], P('expert', None, 'shard')
The draws below stay inside these ranges and needn't reach their ends.
Inputs may be any that keep to these rules, and one draw needn't show every extreme that they name: `expert_ids`: each token names two different experts; among the 64 entries of one device no expert is named more than 20 times, and 20 is reached on some device; every expert is named somewhere.
All inputs are finite; a program needn't handle non-finite values.
Results may differ from the reference program's by a relative error of at most 0.001.
Values may be sent and summed in bfloat16 or wider, within the bound.
A program may use at most 128 MiB of HBM per device.

```python
import math
import jax
import jax.numpy as jnp
import numpy as np
from jax import lax

D = 4096
FF = 8192
BLK = 256
TOK_DEV = 32
EXPERTS = 4
CAP = 20
TOKENS = 1024
N_EXPERT = 4
N_SHARD = 8


def place_ends(values, own_key, least, high):
    longest = values.shape.index(max(values.shape))
    spots = []
    for shift in (0, 1):
        where = [jax.random.randint(jax.random.fold_in(own_key, axis), (), 0, length) for axis, length in enumerate(values.shape)]
        where[longest] = (where[longest] + shift) % values.shape[longest]
        spots.append(tuple(where))
    return values.at[spots[0]].set(least).at[spots[1]].set(high)


def block_scale(rng, dims, cuts, low, high):
    def one(dim, parts):
        steps = jax.random.uniform(jax.random.fold_in(jax.random.fold_in(rng, 6), dim), (parts,), jnp.float32, low / len(cuts), high / len(cuts))
        return jnp.repeat(jnp.exp(steps), dims[dim] // parts).reshape((-1,) + (1,) * (len(dims) - dim - 1))

    loudness = one(*cuts[0])
    for cut in cuts[1:]:
        loudness = loudness * one(*cut)
    return loudness


def assign_block(rng, own, number, rows, count, top, reach, lean):
    sequence = jax.random.permutation(rng, count)
    packed, usual = portions_of(count, rows * top, reach, lean, True), portions_of(count, rows * top, reach, lean, False)
    places = jnp.arange(count)

    def named(tallies, turn):
        used = int((tallies > 0).sum())
        fixed = max(1, used // 4)
        moved = fixed + (places - fixed + turn * (used - fixed)) % max(1, count - fixed)
        return jnp.zeros((count,), jnp.int32).at[sequence[jnp.where(places < fixed, places, moved)]].set(jnp.asarray(tallies, jnp.int32))

    tallies = jnp.where(number % 4 == 0, named(packed, number // 4), named(usual, number - number // 4 - 1))
    mixed = jax.random.permutation(jax.random.fold_in(own, 3), count)
    giver, sink = mixed[0:count // 2 * 2:2], mixed[1:count // 2 * 2:2]
    room = jnp.minimum(tallies[giver] - 1, reach - tallies[sink]) // 2
    room = jnp.where((giver == sequence[0]) | (sink == sequence[0]) | (tallies[sink] == 0), 0, jnp.maximum(room, 0))
    moved = jax.random.randint(jax.random.fold_in(own, 4), (count // 2,), 0, 1 << 20) % (room + 1)
    tallies = tallies.at[giver].add(-moved).at[sink].add(moved)
    members = jnp.searchsorted(jnp.cumsum(tallies), jnp.arange(rows * top), side="right").astype(jnp.int32)
    grid = members.reshape(top, rows).T
    grid = grid[jax.random.permutation(jax.random.fold_in(own, 1), rows)]
    turn = jax.random.randint(jax.random.fold_in(own, 2), (rows, 1), 0, top)
    return jnp.take_along_axis(grid, (jnp.arange(top)[None, :] + turn) % top, axis=1)


def portions_of(count, total, bound, slope, full):
    loads = [(1 << 20) // math.isqrt(rank ** slope) + 1 for rank in range(1, count + 1)]
    largest = bound if full else min(bound, max(-(-total // count), total * loads[0] // sum(loads)))
    least = 1 if total - largest >= count - 1 else 0
    counts, spare = [largest] + [least] * (count - 1), total - largest - least * (count - 1)
    while spare > 0:
        movable = [i for i in range(1, count) if counts[i] < largest] or [i for i in range(1, count) if counts[i] < bound]
        whole, remaining = sum([loads[i] for i in movable]), spare
        for i in movable:
            addition = min(bound - counts[i], max(1, remaining * loads[i] // whole), spare)
            counts[i] = counts[i] + addition
            spare = spare - addition
    return np.array(counts)


def normal_values(own_key, shape, scale, bound, shards=(), held_as=jnp.bfloat16):
    values = scale * jax.random.normal(own_key, shape, jnp.float32)
    if shards:
        values = values * block_scale(own_key, shape, shards, -0.22, 0.18)
    return jnp.clip(values, -bound, bound).astype(held_as)


def setup_inputs(seed: int = 0) -> dict:
    splits = jax.random.split(jax.random.key(seed), 6)
    tokens_in = normal_values(splits[0], (TOKENS, D), 1.0, 6.0, ((0, 32),))
    out_grad = normal_values(splits[1], (TOKENS, 2, FF), 1.0, 6.0, ((0, 32),))
    expert_ids_keys = jax.random.split(jax.random.fold_in(splits[2], 1), TOKENS // TOK_DEV)
    expert_ids_turns = jax.random.permutation(jax.random.fold_in(splits[2], 3), TOKENS // TOK_DEV)
    expert_ids = jax.vmap(lambda own, number: assign_block(jax.random.fold_in(splits[2], 2), own, number, TOK_DEV, EXPERTS, 2, CAP, 2))(expert_ids_keys, expert_ids_turns).reshape((TOKENS, 2))
    d_levels = place_ends(jax.random.randint(splits[3], (EXPERTS, D // BLK), 0, 8), jax.random.fold_in(splits[3], 1), 0, 7).astype(jnp.int32)
    f_levels = place_ends(jax.random.randint(splits[4], (EXPERTS, FF // BLK), 0, 8), jax.random.fold_in(splits[4], 1), 0, 7).astype(jnp.int32)
    return {"tokens_in": tokens_in, "out_grad": out_grad, "expert_ids": expert_ids, "d_levels": d_levels, "f_levels": f_levels}


def invert_blocks(blocks):
    lower = jnp.linalg.cholesky(blocks)
    identity = jnp.eye(blocks.shape[-1], dtype=blocks.dtype)
    return jax.vmap(lambda factor: jax.scipy.linalg.cho_solve((factor, True), identity))(lower)

def damping(levels):
    return 0.05 * jnp.exp(0.4 * levels.astype(jnp.float32))

def reference(tokens_in, out_grad, expert_ids, d_levels, f_levels):
    row_limit = N_EXPERT * N_SHARD * CAP
    flat_ids = expert_ids.reshape(-1)
    tok_index = (jnp.arange(2 * TOKENS, dtype=jnp.int32) // 2).astype(jnp.int32)
    grads_flat = out_grad.reshape(2 * TOKENS, FF)
    highest = lax.Precision.HIGHEST

    def per_expert(inputs):
        expert, d_row, f_row = inputs
        chosen = flat_ids == expert
        ordering = jnp.argsort(jnp.where(chosen, 0, 1).astype(jnp.int32), stable=True)[:row_limit].astype(jnp.int32)
        live_rows = chosen[ordering].astype(jnp.bfloat16)
        row_count = jnp.sum(chosen.astype(jnp.float32))
        x_rows = tokens_in[tok_index[ordering]] * live_rows[:, None]
        g_rows = grads_flat[ordering] * live_rows[:, None]
        gradient = jnp.dot(x_rows.T.astype(jnp.float32), g_rows.astype(jnp.float32), preferred_element_type=jnp.float32)
        x_blocks = x_rows.astype(jnp.float32).reshape(row_limit, D // BLK, BLK)
        g_blocks = g_rows.astype(jnp.float32).reshape(row_limit, FF // BLK, BLK)
        identity = jnp.eye(BLK, dtype=jnp.float32)
        cov_a = jnp.einsum('rbi,rbj->bij', x_blocks, x_blocks, precision=highest) / row_count
        cov_a = cov_a + damping(d_row)[:, None, None] * identity
        cov_f = jnp.einsum('rbi,rbj->bij', g_blocks, g_blocks, precision=highest) / row_count
        cov_f = cov_f + damping(f_row)[:, None, None] * identity
        inv_a = invert_blocks(cov_a)
        inv_f = invert_blocks(cov_f)
        left_done = jnp.einsum('bij,bjf->bif', inv_a, gradient.reshape(D // BLK, BLK, FF), precision=highest)
        precond = jnp.einsum('dcj,cjk->dck', left_done.reshape(D, FF // BLK, BLK), inv_f, precision=highest)
        return precond.reshape(D, FF)
    precond = lax.map(per_expert, (jnp.arange(EXPERTS, dtype=jnp.int32), d_levels, f_levels))
    norm_total = jnp.sum(precond * precond)
    ascent_scale = lax.rsqrt(norm_total / (EXPERTS * D * FF) + 1e-06)
    return (precond * ascent_scale).astype(jnp.bfloat16)
```

```python
import functools

import jax
import jax.numpy as jnp
from jax import lax
from jax.experimental import pallas as pl
from jax.experimental.pallas import tpu as pltpu
from jax.sharding import PartitionSpec as P

BLK = 256
HALF = BLK // 2
MARK = 128
MESH = pl.DeviceIdType.MESH
NN = (((1,), (0,)), ((), ()))
NT = (((1,), (1,)), ((), ()))
TN = (((0,), (0,)), ((), ()))


def dot_f32(a, b, dims=(((1,), (0,)), ((), ()))):
    return lax.dot_general(
        a, b, dims, precision=lax.Precision.HIGHEST, preferred_element_type=jnp.float32
    )


def dot_bf16(a, b, dims=(((1,), (0,)), ((), ()))):
    return lax.dot_general(a, b, dims, preferred_element_type=jnp.float32)


def split(value, parts):
    out = []
    for _ in range(parts):
        part = value.astype(jnp.bfloat16)
        out.append(part)
        value = value - part.astype(jnp.float32)
    return out


def gauss_jordan(work, count):
    lanes = lax.broadcasted_iota(jnp.int32, (HALF, HALF), 1)
    lane_row = lax.broadcasted_iota(jnp.int32, (1, HALF), 1)

    def step(j, carry):
        index = jnp.full((HALF, HALF), j, jnp.int32)
        at_pivot = lanes == j
        matrices = [work[b] for b in range(count)]
        rows = [work[b, pl.ds(j, 1), :] for b in range(count)]
        pivots = [
            jnp.sum(jnp.where(lane_row == j, row, 0.0), axis=1, keepdims=True) for row in rows
        ]
        columns = [jnp.take_along_axis(matrix, index, axis=1) for matrix in matrices]
        scaled = [
            jnp.where(lane_row == j, 1.0, row) / pivot for row, pivot in zip(rows, pivots)
        ]
        updated = [
            jnp.where(at_pivot, 0.0, matrix) - column * row
            for matrix, column, row in zip(matrices, columns, scaled)
        ]
        for b in range(count):
            work[b] = updated[b]
        for b in range(count):
            work[b, pl.ds(j, 1), :] = scaled[b]
        return carry

    lax.fori_loop(0, HALF, step, 0)


def invert_covariances(rows_ref, damp_ref, count_ref, work, cov, aux):
    count = cov.shape[0]
    eye = (
        lax.broadcasted_iota(jnp.int32, (BLK, BLK), 0)
        == lax.broadcasted_iota(jnp.int32, (BLK, BLK), 1)
    )
    for b in range(count):
        rows = rows_ref[:, b * BLK : (b + 1) * BLK]
        product = dot_bf16(rows, rows, TN) / count_ref[0]
        cov[b] = product + jnp.where(eye, damp_ref[b], 0.0)
        work[b] = cov[b, :HALF, :HALF]
    gauss_jordan(work, count)
    for b in range(count):
        first = work[b]
        upper = cov[b, :HALF, HALF:]
        side = dot_f32(first, upper)
        aux[b] = side
        cov[b, :HALF, :HALF] = first
        work[b] = cov[b, HALF:, HALF:] - dot_f32(upper, side, TN)
    gauss_jordan(work, count)
    for b in range(count):
        last = work[b]
        side = aux[b]
        corner = dot_f32(side, last)
        cov[b, :HALF, :HALF] = cov[b, :HALF, :HALF] + dot_f32(corner, side, NT)
        cov[b, :HALF, HALF:] = -corner
        cov[b, HALF:, :HALF] = -corner.T
        cov[b, HALF:, HALF:] = last


def input_kernel(damp_ref, count_ref, rows_ref, inv_ref, work, aux):
    invert_covariances(rows_ref, damp_ref, count_ref, work, inv_ref, aux)


def hidden_kernel(damp_ref, count_ref, rows_ref, high_ref, low_ref, work, aux, cov):
    invert_covariances(rows_ref, damp_ref, count_ref, work, cov, aux)
    for b in range(cov.shape[0]):
        columns = slice(b * BLK, (b + 1) * BLK)
        rows = rows_ref[:, columns]
        total = sum(dot_bf16(rows, part) for part in reversed(split(cov[b], 3)))
        high_ref[:, columns], low_ref[:, columns] = split(total, 2)


def product_kernel(rows_ref, inv_ref, high_ref, low_ref, out_ref, norm_ref):
    rows = rows_ref[0]
    left = sum(dot_bf16(part, rows, NT) for part in reversed(split(inv_ref[0], 3)))
    left_high, left_low = split(left, 2)
    high = high_ref[...]
    out = dot_bf16(left_high, low_ref[...]) + dot_bf16(left_low, high) + dot_bf16(left_high, high)
    out_ref[...] = out

    @pl.when(pl.program_id(0) == 0)
    def _():
        norm_ref[...] = jnp.zeros_like(norm_ref)

    norm_ref[...] += jnp.sum((out * out).reshape(-1, 8, out.shape[1]), axis=0)


def damping(levels):
    return 0.05 * jnp.exp(0.4 * levels.astype(jnp.float32))


def call_blocks(kernel, damp, row_count, rows, out_shape, with_cov):
    count = damp.shape[0]
    scratch = [pltpu.VMEM((count, HALF, HALF), jnp.float32)] * 2
    if with_cov:
        scratch.append(pltpu.VMEM((count, BLK, BLK), jnp.float32))
    vmem = pl.BlockSpec(memory_space=pltpu.VMEM)
    smem = pl.BlockSpec(memory_space=pltpu.SMEM)
    return pl.pallas_call(
        kernel,
        out_shape=out_shape,
        in_specs=[smem, smem, vmem],
        out_specs=jax.tree.map(lambda _: vmem, out_shape),
        scratch_shapes=scratch,
        compiler_params=pltpu.CompilerParams(vmem_limit_bytes=48 << 20),
        cost_estimate=pl.CostEstimate(flops=20_000_000_000, bytes_accessed=4_000_000, transcendentals=0),
    )(damp, row_count, rows)


def plain(tokens_in, out_grad, expert_ids, d_levels, f_levels):
    group_count = lax.axis_size("expert")
    shard_count = lax.axis_size("shard")
    tok_rows = tokens_in.shape[0]
    width = tokens_in.shape[1]
    ff_full = out_grad.shape[2]
    ff_dev = ff_full // shard_count
    width_dev = width // shard_count
    capacity = min(tok_rows, max(2, 5 * tok_rows // (2 * group_count)))
    slot_total = group_count * capacity
    flat_ids = expert_ids.reshape(-1)
    member = (flat_ids[:, None] == jnp.arange(group_count, dtype=jnp.int32)[None, :]).astype(
        jnp.int32
    )
    before = jnp.cumsum(member, axis=0) - member
    ranking = jnp.sum(before * member, axis=1)
    target = flat_ids * capacity + ranking
    dispatch = (jnp.arange(slot_total, dtype=jnp.int32)[:, None] == target[None, :]).astype(
        jnp.bfloat16
    )
    per_token = jnp.sum(
        dispatch.reshape(slot_total, tok_rows, 2).astype(jnp.float32), axis=2
    ).astype(jnp.bfloat16)
    x_send = jnp.dot(per_token, tokens_in, preferred_element_type=jnp.float32).astype(jnp.bfloat16)
    g_send = jnp.dot(
        dispatch, out_grad.reshape(2 * tok_rows, ff_full), preferred_element_type=jnp.float32
    ).astype(jnp.bfloat16)
    valid_slot = jnp.sum(dispatch.astype(jnp.float32), axis=1).astype(jnp.bfloat16)
    send = jnp.concatenate(
        (
            x_send.reshape(group_count, capacity, shard_count, width_dev),
            g_send.reshape(group_count, capacity, shard_count, ff_dev),
            jnp.broadcast_to(
                valid_slot.reshape(group_count, capacity, 1, 1),
                (group_count, capacity, shard_count, MARK),
            ),
        ),
        axis=3,
    )
    send = send.transpose(0, 2, 1, 3).reshape(group_count * shard_count, capacity, -1)
    rows = lax.all_to_all(send, ("expert", "shard"), split_axis=0, concat_axis=0, tiled=True)
    rows = rows.reshape(-1, rows.shape[2])
    own_x = rows[:, :width_dev]
    rows_g = rows[:, width_dev : width_dev + ff_dev]
    row_count = jnp.sum(rows[:, width_dev + ff_dev].astype(jnp.float32)).reshape(1)
    row_total = rows.shape[0]
    rows_x = lax.all_gather(own_x, "shard", axis=0)

    own_blocks = width_dev // BLK
    first_block = lax.axis_index("shard") * own_blocks
    own_levels = lax.dynamic_slice_in_dim(d_levels[0], first_block, own_blocks, 0)
    inv_a = call_blocks(
        input_kernel,
        damping(own_levels),
        row_count,
        own_x,
        jax.ShapeDtypeStruct((own_blocks, BLK, BLK), jnp.float32),
        False,
    )
    inv_a = lax.all_gather(inv_a, "shard", axis=0, tiled=True)
    half = jax.ShapeDtypeStruct((row_total, ff_dev), jnp.bfloat16)
    g_high, g_low = call_blocks(
        hidden_kernel, damping(f_levels[0]), row_count, rows_g, (half, half), True
    )
    blocks = width // BLK
    whole = pl.BlockSpec((row_total, ff_dev), lambda b: (0, 0))
    precond, squares = pl.pallas_call(
        product_kernel,
        grid=(blocks,),
        out_shape=(
            jax.ShapeDtypeStruct((width, ff_dev), jnp.float32),
            jax.ShapeDtypeStruct((8, ff_dev), jnp.float32),
        ),
        in_specs=[
            pl.BlockSpec((1, row_total, BLK), lambda b: (b // own_blocks, 0, b % own_blocks)),
            pl.BlockSpec((1, BLK, BLK), lambda b: (b, 0, 0)),
            whole,
            whole,
        ],
        out_specs=(
            pl.BlockSpec((BLK, ff_dev), lambda b: (b, 0)),
            pl.BlockSpec((8, ff_dev), lambda b: (0, 0)),
        ),
        compiler_params=pltpu.CompilerParams(
            dimension_semantics=("arbitrary",), vmem_limit_bytes=48 << 20
        ),
        cost_estimate=pl.CostEstimate(
            flops=6 * row_total * width * ff_dev, bytes_accessed=4 * width * ff_dev, transcendentals=0
        ),
    )(rows_x, inv_a, g_high, g_low)
    norm_total = lax.psum(jnp.sum(squares), ("expert", "shard"))
    ascent_scale = lax.rsqrt(norm_total / (group_count * width * ff_full) + 1e-06)
    return (precond * ascent_scale).astype(jnp.bfloat16)[None]


def comm_kernel(group, shards, pair, x_ref, m_ref, xall, rall, zs, ys, xs, ps, gs, xr, gr, local):
    expert = lax.axis_index("expert")
    shard = lax.axis_index("shard")
    chip_x, core = expert // 2, lax.rem(expert, 2)
    depth = shards // pair
    z, y = shard // pair, lax.rem(shard, pair)
    cols = xall.shape[3]
    me = expert * shards + shard

    def place(px, py, pz, pc):
        return (px * 2 + pc, pz * pair + py)

    def number(px, py, pz, pc):
        return (px * 2 + pc) * shards + pz * pair + py

    others = [
        (lax.rem(expert + de, group), lax.rem(shard + ds, shards))
        for ds in range(shards)
        for de in range(group)
        if de or ds
    ]
    barrier = pltpu.get_barrier_semaphore()
    for other in others:
        pl.semaphore_signal(barrier, 1, device_id=other, device_id_type=MESH)
    pl.semaphore_wait(barrier, len(others))

    pending = []

    def send(valid, source, unit, half, target, sem):
        copy = pltpu.make_async_remote_copy(
            src_ref=source,
            dst_ref=xall.at[half, unit],
            send_sem=sem,
            recv_sem=xr.at[unit * 2 + half],
            device_id=target,
            device_id_type=MESH,
        )
        pl.when(valid)(copy.start)
        pending.append((valid, copy))

    def arrive(valid, unit, half):
        @pl.when(valid)
        def _():
            pltpu.make_async_remote_copy(
                src_ref=xall.at[half, unit],
                dst_ref=xall.at[half, unit],
                send_sem=zs.at[0],
                recv_sem=xr.at[unit * 2 + half],
                device_id=(expert, shard),
                device_id_type=MESH,
            ).wait_recv()

    def along_z(valid, up, k, half):
        origin = z - k if up else z + k
        unit = number(chip_x, y, origin, core)
        source = x_ref.at[:, pl.ds(half * cols, cols)] if k == 0 else xall.at[half, unit]
        more = jnp.logical_and(valid, z < depth - 1 if up else z > 0)
        step = 1 if up else -1
        send(more, source, unit, half, place(chip_x, y, z + step, core), zs.at[(k * 2 + half) * 2 + int(up)])

    def spread(valid, origin, k, half):
        unit = number(chip_x, y, origin, core)
        source = x_ref.at[:, pl.ds(half * cols, cols)] if k == 0 else xall.at[half, unit]
        send(valid, source, unit, half, place(chip_x, 1 - y, z, core), ys.at[origin * 2 + half])
        send(valid, source, unit, half, place(1 - chip_x, y, z, core), xs.at[origin * 2 + half])
        send(valid, source, unit, half, place(chip_x, y, z, 1 - core), ps.at[((0 * 2 + 0) * depth + origin) * 2 + half])

    def second(valid, origin, half):
        if half == 0:
            unit = number(chip_x, 1 - y, origin, core)
        else:
            unit = number(1 - chip_x, y, origin, core)
        arrive(valid, unit, half)
        source = xall.at[half, unit]
        if half == 0:
            send(valid, source, unit, half, place(1 - chip_x, y, z, core), xs.at[2 * depth + origin])
        else:
            send(valid, source, unit, half, place(chip_x, 1 - y, z, core), ys.at[2 * depth + origin])
        send(valid, source, unit, half, place(chip_x, y, z, 1 - core), ps.at[((0 * 2 + 1) * depth + origin) * 2 + half])

    def third(valid, origin, half):
        near = number(1 - chip_x, y, origin, core) if half == 0 else number(chip_x, 1 - y, origin, core)
        far = number(1 - chip_x, 1 - y, origin, core)
        for row, unit in enumerate((near, far)):
            arrive(valid, unit, half)
            send(valid, xall.at[half, unit], unit, half, place(chip_x, y, z, 1 - core), ps.at[((1 * 2 + row) * depth + origin) * 2 + half])

    always = z >= 0
    own = pltpu.make_async_copy(m_ref.at[me], rall.at[me], local.at[2])
    own.start()
    keeps = []
    for half in range(2):
        keep = pltpu.make_async_copy(x_ref.at[:, pl.ds(half * cols, cols)], xall.at[half, me], local.at[half])
        keep.start()
        keeps.append(keep)
        along_z(always, True, 0, half)
        along_z(always, False, 0, half)
    for half in range(2):
        spread(always, z, 0, half)

    def messages(part):
        for i, other in enumerate(others):
            if i % 3 != part:
                continue
            there = other[0] * shards + other[1]
            copy = pltpu.make_async_remote_copy(
                src_ref=m_ref.at[there],
                dst_ref=rall.at[me],
                send_sem=gs.at[i],
                recv_sem=gr.at[me],
                device_id=other,
                device_id_type=MESH,
            )
            copy.start()
            pending.append((always, copy))

    for k in range(depth + 2):
        if 1 <= k < depth:
            for half in range(2):
                for up in (True, False):
                    origin = z - k if up else z + k
                    valid = z >= k if up else z + k <= depth - 1
                    arrive(valid, number(chip_x, y, origin, core), half)
                    along_z(valid, up, k, half)
            for half in range(2):
                for up in (True, False):
                    origin = z - k if up else z + k
                    valid = z >= k if up else z + k <= depth - 1
                    spread(valid, origin, k, half)
            messages(k - 1)
        if 1 <= k <= depth:
            j = k - 1
            for half in range(2):
                if j == 0:
                    second(always, z, half)
                else:
                    second(z >= j, z - j, half)
                    second(z + j <= depth - 1, z + j, half)
        if k >= 2:
            j = k - 2
            for half in range(2):
                if j == 0:
                    third(always, z, half)
                else:
                    third(z >= j, z - j, half)
                    third(z + j <= depth - 1, z + j, half)
    for px in range(2):
        for py in range(pair):
            for pz in range(depth):
                for half in range(2):
                    arrive(always, number(px, py, pz, 1 - core), half)
    for other in others:
        there = other[0] * shards + other[1]
        pltpu.make_async_remote_copy(
            src_ref=m_ref.at[there],
            dst_ref=rall.at[there],
            send_sem=gs.at[0],
            recv_sem=gr.at[there],
            device_id=(expert, shard),
            device_id_type=MESH,
        ).wait_recv()
    for valid, copy in pending:
        pl.when(valid)(copy.wait_send)
    own.wait()
    for keep in keeps:
        keep.wait()


def exchange(tokens, messages, group, shards):
    total = group * shards
    rows, width = tokens.shape
    pair = group // 2
    depth = shards // pair
    dma = pltpu.SemaphoreType.DMA
    anywhere = pl.BlockSpec(memory_space=pl.ANY)
    return pl.pallas_call(
        functools.partial(comm_kernel, group, shards, pair),
        out_shape=(
            jax.ShapeDtypeStruct((2, total, rows, width // 2), tokens.dtype),
            jax.ShapeDtypeStruct(messages.shape, messages.dtype),
        ),
        in_specs=[pl.BlockSpec(memory_space=pltpu.VMEM), pl.BlockSpec(memory_space=pltpu.VMEM)],
        out_specs=(anywhere, anywhere),
        scratch_shapes=[
            dma((4 * depth,)),
            dma((3 * depth,)),
            dma((3 * depth,)),
            dma((8 * depth,)),
            dma((total,)),
            dma((2 * total,)),
            dma((total,)),
            dma((3,)),
        ],
        compiler_params=pltpu.CompilerParams(collective_id=0, has_side_effects=True),
    )(tokens, messages)


def leaf_inverse(work, unroll):
    packs, size, lanes = work.shape
    lane = lax.broadcasted_iota(jnp.int32, (8, lanes), 1)
    inner = lax.rem(lane, size)
    base = lane - inner

    def step(i, carry):
        j = i * 2
        at0, at1 = inner == j, inner == j + 1
        index0, index1 = base + j, base + j + 1
        pivot = jnp.logical_or(at0, at1)
        take = lambda v, ix: jnp.take_along_axis(v, ix, axis=1)
        news = []
        for p in range(packs):
            r0 = jnp.broadcast_to(work[p, pl.ds(j, 1), :], (8, lanes))
            r1 = jnp.broadcast_to(work[p, pl.ds(j + 1, 1), :], (8, lanes))
            a, b = take(r0, index0), take(r0, index1)
            c, d = take(r1, index0), take(r1, index1)
            scale = 1.0 / (a * d - b * c)
            r0 = jnp.where(at0, 1.0, jnp.where(at1, 0.0, r0))
            r1 = jnp.where(at1, 1.0, jnp.where(at0, 0.0, r1))
            news.append(((d * scale) * r0 - (b * scale) * r1, (a * scale) * r1 - (c * scale) * r0))
        for p in range(packs):
            s0, s1 = news[p]
            for t in range(size // 8):
                m = work[p, t * 8:(t + 1) * 8, :]
                c0, c1 = take(m, index0), take(m, index1)
                work[p, t * 8:(t + 1) * 8, :] = jnp.where(pivot, 0.0, m) - c0 * s0 - c1 * s1
        for p in range(packs):
            s0, s1 = news[p]
            work[p, pl.ds(j, 1), :] = s0[:1]
            work[p, pl.ds(j + 1, 1), :] = s1[:1]
        return carry

    lax.fori_loop(0, size // 2, step, 0, unroll=unroll)

def invert(cov, work, side_ref, mid_ref, low_ref, leaf=64, unroll=False):
    count, full, _ = cov.shape
    per = 128 // leaf

    def solve_leaf(offset):
        for p in range(count // per):
            parts = [cov[p * per + i, offset:offset + leaf, offset:offset + leaf] for i in range(per)]
            work[p] = jnp.concatenate(parts, axis=1) if per > 1 else parts[0]
        leaf_inverse(work, unroll)
        for p in range(count // per):
            for i in range(per):
                cov[p * per + i, offset:offset + leaf, offset:offset + leaf] = work[p][:, i * leaf:(i + 1) * leaf]

    def solve(offset, size):
        if size == leaf:
            solve_leaf(offset)
            return
        half = size // 2
        one, two = slice(offset, offset + half), slice(offset + half, offset + size)
        solve(offset, half)
        store = side_ref if size == full else mid_ref if size == full // 2 else low_ref
        for n in range(count):
            upper = cov[n, one, two]
            side = dot_f32(cov[n, one, one], upper)
            store[n] = side
            cov[n, two, two] = cov[n, two, two] - dot_f32(upper, side, TN)
        solve(offset + half, half)
        for n in range(count):
            last = cov[n, two, two]
            side = store[n]
            corner = dot_f32(side, last)
            cov[n, one, one] = cov[n, one, one] + dot_f32(corner, side, NT)
            cov[n, one, two] = -corner
            cov[n, two, one] = -corner.T
    solve(0, full)


def same(shape, rows, columns):
    return rows(lax.broadcasted_iota(jnp.int32, shape, 0)) == columns(lax.broadcasted_iota(jnp.int32, shape, 1))


def one_hot(mask):
    return jnp.where(mask, 1.0, 0.0).astype(jnp.bfloat16)


def inverse_kernel(
    main, tokens, damp_a, damp_f, x_ref, m_ref, xc_ref, gc_ref, ahi_ref, alo_ref, shi_ref, slo_ref, cov, work, side, mid, low
):
    sources = m_ref.shape[0]
    ff = gc_ref.shape[1]
    blocks = ff // BLK
    extra = main // blocks
    batch = BLK // tokens
    groups = sources // batch
    rows_main, rows_extra = batch * main, batch * extra
    rows_all = rows_main + rows_extra
    width = x_ref.shape[2]
    tile_main = one_hot(same((MARK, BLK), lambda i: i, lambda j: lax.rem(j, tokens)))
    tile_extra = one_hot(same((MARK, BLK), lambda i: i - tokens, lambda j: lax.rem(j, tokens)))
    owner = same((rows_main, BLK), lambda i: i // main, lambda j: j // tokens)
    first = one_hot(same((rows_extra, rows_main), lambda i: (i // extra) * main + lax.rem(i, extra), lambda j: j))
    total = jnp.zeros((), jnp.float32)
    for g in range(groups):
        part = m_ref[g * batch : (g + 1) * batch].reshape(rows_main, -1)
        marks = part[:, ff + BLK :]
        pick = jnp.where(owner, dot_bf16(marks, tile_main), 0.0)
        rest = jnp.where(owner, dot_bf16(marks, tile_extra), 0.0).astype(jnp.bfloat16)
        rest = dot_bf16(first, rest)
        total = total + jnp.sum(pick) + jnp.sum(rest)
        pick, rest = pick.astype(jnp.bfloat16), rest.astype(jnp.bfloat16)
        base = g * rows_all
        for h in range(2):
            rows = x_ref[h, g * BLK : (g + 1) * BLK, :]
            xc_ref[base : base + rows_main, h * width : (h + 1) * width] = dot_bf16(pick, rows).astype(jnp.bfloat16)
            xc_ref[base + rows_main : base + rows_all, h * width : (h + 1) * width] = dot_bf16(rest, rows).astype(
                jnp.bfloat16
            )
        gc_ref[base : base + rows_main, :] = part[:, :ff]
        for q in range(blocks):
            chosen = one_hot(
                same((rows_extra, rows_main), lambda i: (i // extra) * main + q * extra + lax.rem(i, extra), lambda j: j)
            )
            gc_ref[base + rows_main : base + rows_all, q * BLK : (q + 1) * BLK] = dot_bf16(
                chosen, part[:, ff : ff + BLK]
            ).astype(jnp.bfloat16)
    scale = 1.0 / jnp.broadcast_to(total, (1, 1))
    eye = same((BLK, BLK), lambda i: i, lambda j: j)
    count_a = ahi_ref.shape[0]
    for b in range(count_a):
        rows = xc_ref[:, b * BLK : (b + 1) * BLK]
        cov[b] = dot_bf16(rows, rows, TN) * scale + jnp.where(eye, damp_a[b], 0.0)
    for b in range(blocks):
        rows = gc_ref[:, b * BLK : (b + 1) * BLK]
        cov[count_a + b] = dot_bf16(rows, rows, TN) * scale + jnp.where(eye, damp_f[b], 0.0)
    invert(cov, work, side, mid, low)
    for b in range(count_a):
        ahi_ref[b], alo_ref[b] = split(cov[b], 2)
    for b in range(blocks):
        shi_ref[b], slo_ref[b] = split(cov[count_a + b], 2)


def three(a, b, dims=NN):
    return dot_bf16(a[0], b[1], dims) + dot_bf16(a[1], b[0], dims) + dot_bf16(a[0], b[0], dims)


def precond_kernel(x_ref, g_ref, ahi_ref, alo_ref, shi_ref, slo_ref, out_ref, norm_ref):
    gradient = dot_bf16(x_ref[...], g_ref[...], TN)
    left = (ahi_ref[0], alo_ref[0])

    @pl.when(pl.program_id(0) == 0)
    def _():
        norm_ref[...] = jnp.zeros_like(norm_ref)

    for c in range(shi_ref.shape[0]):
        columns = slice(c * BLK, (c + 1) * BLK)
        right = three(split(gradient[:, columns], 2), (shi_ref[c], slo_ref[c]))
        out = three(left, split(right, 2))
        out_ref[:, columns] = out
        norm_ref[:, columns] += jnp.sum((out * out).reshape(-1, 8, BLK), axis=0)


def total_kernel(group, shards, scale, part_ref, out_ref, parts, send_sem, recv_sem):
    expert = lax.axis_index("expert")
    shard = lax.axis_index("shard")
    me = expert * shards + shard
    others = [
        (lax.rem(expert + de, group), lax.rem(shard + ds, shards))
        for ds in range(shards)
        for de in range(group)
        if de or ds
    ]
    barrier = pltpu.get_barrier_semaphore()
    for other in others:
        pl.semaphore_signal(barrier, 1, device_id=other, device_id_type=MESH)
    pl.semaphore_wait(barrier, len(others))
    copies = []
    for i, other in enumerate(others):
        copy = pltpu.make_async_remote_copy(
            src_ref=part_ref,
            dst_ref=parts.at[me],
            send_sem=send_sem.at[i],
            recv_sem=recv_sem.at[me],
            device_id=other,
            device_id_type=MESH,
        )
        copy.start()
        copies.append(copy)
    parts[me] = part_ref[...]
    for other in others:
        there = other[0] * shards + other[1]
        pltpu.make_async_remote_copy(
            src_ref=part_ref,
            dst_ref=parts.at[there],
            send_sem=send_sem.at[0],
            recv_sem=recv_sem.at[there],
            device_id=(expert, shard),
            device_id_type=MESH,
        ).wait_recv()
    total = jnp.sum(jnp.sum(parts[...], axis=0))
    out_ref[...] = lax.rsqrt(jnp.broadcast_to(total, out_ref.shape) * scale + 1e-06)
    for copy in copies:
        copy.wait_send()


def total_scale(part, group, shards, entries):
    total = group * shards
    dma = pltpu.SemaphoreType.DMA
    vmem = pl.BlockSpec(memory_space=pltpu.VMEM)
    return pl.pallas_call(
        functools.partial(total_kernel, group, shards, 1.0 / entries),
        out_shape=jax.ShapeDtypeStruct((8, 128), jnp.float32),
        in_specs=[vmem],
        out_specs=vmem,
        scratch_shapes=[pltpu.VMEM((total, 8, 128), jnp.float32), dma((total,)), dma((total,))],
        compiler_params=pltpu.CompilerParams(collective_id=1, has_side_effects=True),
    )(part)


def capacity_of(tok_rows, group_count):
    return min(tok_rows, max(2, 5 * tok_rows // (2 * group_count)))


def fast(tokens_in, out_grad, expert_ids, d_levels, f_levels):
    group_count = lax.axis_size("expert")
    shard_count = lax.axis_size("shard")
    tok_rows, width = tokens_in.shape
    ff_full = out_grad.shape[2]
    ff_dev = ff_full // shard_count
    blocks = ff_dev // BLK
    count_a = width // BLK
    capacity = capacity_of(tok_rows, group_count)
    main = 16 * (capacity // 16)
    extra = capacity - main
    total = group_count * shard_count
    flat_ids = expert_ids.reshape(-1)
    member = (flat_ids[:, None] == jnp.arange(group_count, dtype=jnp.int32)[None, :]).astype(jnp.int32)
    before = jnp.cumsum(member, axis=0) - member
    ranking = jnp.sum(before * member, axis=1)
    target = flat_ids * capacity + ranking
    dispatch = (jnp.arange(group_count * capacity, dtype=jnp.int32)[:, None] == target[None, :]).astype(jnp.bfloat16)
    per_token = jnp.sum(dispatch.reshape(-1, tok_rows, 2).astype(jnp.float32), axis=2).astype(jnp.bfloat16)
    sent = jnp.dot(dispatch, out_grad.reshape(2 * tok_rows, ff_full), preferred_element_type=jnp.float32)
    sent = sent.astype(jnp.bfloat16).reshape(group_count, capacity, ff_full)
    marks = per_token.reshape(group_count, capacity, tok_rows)
    first = sent[:, :main].reshape(group_count, main, shard_count, ff_dev).transpose(0, 2, 1, 3)
    last = sent[:, main:].reshape(group_count, extra, shard_count, blocks, BLK).transpose(0, 2, 3, 1, 4)
    info = jnp.concatenate(
        (
            marks[:, :main],
            jnp.pad(marks[:, main:], ((0, 0), (0, main - extra), (0, 0))),
            jnp.zeros((group_count, main, MARK - 2 * tok_rows), jnp.bfloat16),
        ),
        axis=2,
    )
    messages = jnp.concatenate(
        (
            first.reshape(total, main, ff_dev),
            last.reshape(total, main, BLK),
            jnp.broadcast_to(info[:, None], (group_count, shard_count, main, MARK)).reshape(total, main, MARK),
        ),
        axis=2,
    )
    rows_x, rows_m = exchange(tokens_in, messages, group_count, shard_count)
    rows_x = rows_x.reshape(2, total * tok_rows, width // 2)

    row_total = total * capacity
    count = count_a + blocks
    vmem = pl.BlockSpec(memory_space=pltpu.VMEM)
    smem = pl.BlockSpec(memory_space=pltpu.SMEM)
    f32 = jnp.float32
    xc, gc, ahi, alo, shi, slo = pl.pallas_call(
        functools.partial(inverse_kernel, main, tok_rows),
        out_shape=(
            jax.ShapeDtypeStruct((row_total, width), jnp.bfloat16),
            jax.ShapeDtypeStruct((row_total, ff_dev), jnp.bfloat16),
            jax.ShapeDtypeStruct((count_a, BLK, BLK), jnp.bfloat16),
            jax.ShapeDtypeStruct((count_a, BLK, BLK), jnp.bfloat16),
            jax.ShapeDtypeStruct((blocks, BLK, BLK), jnp.bfloat16),
            jax.ShapeDtypeStruct((blocks, BLK, BLK), jnp.bfloat16),
        ),
        in_specs=[smem, smem, vmem, vmem],
        out_specs=(vmem,) * 6,
        scratch_shapes=[
            pltpu.VMEM((count, BLK, BLK), f32),
            pltpu.VMEM((count // 2, 64, 128), f32),
            pltpu.VMEM((count, HALF, HALF), f32),
            pltpu.VMEM((count, HALF // 2, HALF // 2), f32),
            pltpu.VMEM((count, HALF // 4, HALF // 4), f32),
        ],
        compiler_params=pltpu.CompilerParams(vmem_limit_bytes=48 << 20),
    )(damping(d_levels[0]), damping(f_levels[0]), rows_x, rows_m)

    precond, squares = pl.pallas_call(
        precond_kernel,
        grid=(count_a,),
        out_shape=(
            jax.ShapeDtypeStruct((width, ff_dev), f32),
            jax.ShapeDtypeStruct((8, ff_dev), f32),
        ),
        in_specs=[
            pl.BlockSpec((row_total, BLK), lambda b: (0, b)),
            pl.BlockSpec((row_total, ff_dev), lambda b: (0, 0)),
            pl.BlockSpec((1, BLK, BLK), lambda b: (b, 0, 0)),
            pl.BlockSpec((1, BLK, BLK), lambda b: (b, 0, 0)),
            pl.BlockSpec((blocks, BLK, BLK), lambda b: (0, 0, 0)),
            pl.BlockSpec((blocks, BLK, BLK), lambda b: (0, 0, 0)),
        ],
        out_specs=(
            pl.BlockSpec((BLK, ff_dev), lambda b: (b, 0)),
            pl.BlockSpec((8, ff_dev), lambda b: (0, 0)),
        ),
        compiler_params=pltpu.CompilerParams(dimension_semantics=("arbitrary",), vmem_limit_bytes=32 << 20),
    )(xc, gc, ahi, alo, shi, slo)
    part = jnp.sum(squares.reshape(8, -1, 128), axis=1)
    scale = total_scale(part, group_count, shard_count, group_count * width * ff_full)
    return (precond * scale[0, 0]).astype(jnp.bfloat16)[None]


def local(tokens_in, out_grad, expert_ids, d_levels, f_levels):
    group_count = lax.axis_size("expert")
    shard_count = lax.axis_size("shard")
    tok_rows, width = tokens_in.shape
    blocks = out_grad.shape[2] // shard_count // BLK
    main = 16 * (capacity_of(tok_rows, group_count) // 16)
    extra = capacity_of(tok_rows, group_count) - main
    chips = group_count // 2 == 2 and shard_count % 2 == 0
    packed = main > 0 and extra * blocks == main and 2 * tok_rows <= MARK and BLK % tok_rows == 0
    even = (group_count * shard_count * tok_rows) % BLK == 0 and (width // BLK + blocks) % 2 == 0
    small = group_count * shard_count * tok_rows * width * 2 <= 12 << 20
    if chips and packed and even and small:
        return fast(tokens_in, out_grad, expert_ids, d_levels, f_levels)
    return plain(tokens_in, out_grad, expert_ids, d_levels, f_levels)


def solution(mesh):
    return jax.shard_map(
        local,
        mesh=mesh,
        in_specs=(
            P(("expert", "shard"), None),
            P(("expert", "shard"), None, None),
            P(("expert", "shard"), None),
            P("expert", None),
            P("expert", "shard"),
        ),
        out_specs=P("expert", None, "shard"),
        check_vma=False,
    )
```

```python
import functools

import jax
import jax.numpy as jnp
from jax import lax
from jax.experimental import pallas as pl
from jax.experimental.pallas import tpu as pltpu
from jax.sharding import PartitionSpec as P

BLK = 256
HALF = BLK // 2
MARK = 128
LEAF = 64
MESH = pl.DeviceIdType.MESH
NN = (((1,), (0,)), ((), ()))
NT = (((1,), (1,)), ((), ()))
TN = (((0,), (0,)), ((), ()))


def dot_f32(a, b, dims=(((1,), (0,)), ((), ()))):
    return lax.dot_general(
        a, b, dims, precision=lax.Precision.HIGHEST, preferred_element_type=jnp.float32
    )


def dot_bf16(a, b, dims=(((1,), (0,)), ((), ()))):
    return lax.dot_general(a, b, dims, preferred_element_type=jnp.float32)


def split(value, parts):
    out = []
    for _ in range(parts):
        part = value.astype(jnp.bfloat16)
        out.append(part)
        value = value - part.astype(jnp.float32)
    return out


def gauss_jordan(work, count):
    lanes = lax.broadcasted_iota(jnp.int32, (HALF, HALF), 1)
    lane_row = lax.broadcasted_iota(jnp.int32, (1, HALF), 1)

    def step(j, carry):
        index = jnp.full((HALF, HALF), j, jnp.int32)
        at_pivot = lanes == j
        matrices = [work[b] for b in range(count)]
        rows = [work[b, pl.ds(j, 1), :] for b in range(count)]
        pivots = [
            jnp.sum(jnp.where(lane_row == j, row, 0.0), axis=1, keepdims=True) for row in rows
        ]
        columns = [jnp.take_along_axis(matrix, index, axis=1) for matrix in matrices]
        scaled = [
            jnp.where(lane_row == j, 1.0, row) / pivot for row, pivot in zip(rows, pivots)
        ]
        updated = [
            jnp.where(at_pivot, 0.0, matrix) - column * row
            for matrix, column, row in zip(matrices, columns, scaled)
        ]
        for b in range(count):
            work[b] = updated[b]
        for b in range(count):
            work[b, pl.ds(j, 1), :] = scaled[b]
        return carry

    lax.fori_loop(0, HALF, step, 0)


def invert_covariances(rows_ref, damp_ref, count_ref, work, cov, aux):
    count = cov.shape[0]
    eye = (
        lax.broadcasted_iota(jnp.int32, (BLK, BLK), 0)
        == lax.broadcasted_iota(jnp.int32, (BLK, BLK), 1)
    )
    for b in range(count):
        rows = rows_ref[:, b * BLK : (b + 1) * BLK]
        product = dot_bf16(rows, rows, TN) / count_ref[0]
        cov[b] = product + jnp.where(eye, damp_ref[b], 0.0)
        work[b] = cov[b, :HALF, :HALF]
    gauss_jordan(work, count)
    for b in range(count):
        first = work[b]
        upper = cov[b, :HALF, HALF:]
        side = dot_f32(first, upper)
        aux[b] = side
        cov[b, :HALF, :HALF] = first
        work[b] = cov[b, HALF:, HALF:] - dot_f32(upper, side, TN)
    gauss_jordan(work, count)
    for b in range(count):
        last = work[b]
        side = aux[b]
        corner = dot_f32(side, last)
        cov[b, :HALF, :HALF] = cov[b, :HALF, :HALF] + dot_f32(corner, side, NT)
        cov[b, :HALF, HALF:] = -corner
        cov[b, HALF:, :HALF] = -corner.T
        cov[b, HALF:, HALF:] = last


def input_kernel(damp_ref, count_ref, rows_ref, inv_ref, work, aux):
    invert_covariances(rows_ref, damp_ref, count_ref, work, inv_ref, aux)


def hidden_kernel(damp_ref, count_ref, rows_ref, high_ref, low_ref, work, aux, cov):
    invert_covariances(rows_ref, damp_ref, count_ref, work, cov, aux)
    for b in range(cov.shape[0]):
        columns = slice(b * BLK, (b + 1) * BLK)
        rows = rows_ref[:, columns]
        total = sum(dot_bf16(rows, part) for part in reversed(split(cov[b], 3)))
        high_ref[:, columns], low_ref[:, columns] = split(total, 2)


def product_kernel(rows_ref, inv_ref, high_ref, low_ref, out_ref, norm_ref):
    rows = rows_ref[0]
    left = sum(dot_bf16(part, rows, NT) for part in reversed(split(inv_ref[0], 3)))
    left_high, left_low = split(left, 2)
    high = high_ref[...]
    out = dot_bf16(left_high, low_ref[...]) + dot_bf16(left_low, high) + dot_bf16(left_high, high)
    out_ref[...] = out

    @pl.when(pl.program_id(0) == 0)
    def _():
        norm_ref[...] = jnp.zeros_like(norm_ref)

    norm_ref[...] += jnp.sum((out * out).reshape(-1, 8, out.shape[1]), axis=0)


def damping(levels):
    return 0.05 * jnp.exp(0.4 * levels.astype(jnp.float32))


def call_blocks(kernel, damp, row_count, rows, out_shape, with_cov):
    count = damp.shape[0]
    scratch = [pltpu.VMEM((count, HALF, HALF), jnp.float32)] * 2
    if with_cov:
        scratch.append(pltpu.VMEM((count, BLK, BLK), jnp.float32))
    vmem = pl.BlockSpec(memory_space=pltpu.VMEM)
    smem = pl.BlockSpec(memory_space=pltpu.SMEM)
    return pl.pallas_call(
        kernel,
        out_shape=out_shape,
        in_specs=[smem, smem, vmem],
        out_specs=jax.tree.map(lambda _: vmem, out_shape),
        scratch_shapes=scratch,
        compiler_params=pltpu.CompilerParams(vmem_limit_bytes=48 << 20),
        cost_estimate=pl.CostEstimate(flops=20_000_000_000, bytes_accessed=4_000_000, transcendentals=0),
    )(damp, row_count, rows)


def plain(tokens_in, out_grad, expert_ids, d_levels, f_levels):
    group_count = lax.axis_size("expert")
    shard_count = lax.axis_size("shard")
    tok_rows = tokens_in.shape[0]
    width = tokens_in.shape[1]
    ff_full = out_grad.shape[2]
    ff_dev = ff_full // shard_count
    width_dev = width // shard_count
    capacity = min(tok_rows, max(2, 5 * tok_rows // (2 * group_count)))
    slot_total = group_count * capacity
    flat_ids = expert_ids.reshape(-1)
    member = (flat_ids[:, None] == jnp.arange(group_count, dtype=jnp.int32)[None, :]).astype(
        jnp.int32
    )
    before = jnp.cumsum(member, axis=0) - member
    ranking = jnp.sum(before * member, axis=1)
    target = flat_ids * capacity + ranking
    dispatch = (jnp.arange(slot_total, dtype=jnp.int32)[:, None] == target[None, :]).astype(
        jnp.bfloat16
    )
    per_token = jnp.sum(
        dispatch.reshape(slot_total, tok_rows, 2).astype(jnp.float32), axis=2
    ).astype(jnp.bfloat16)
    x_send = jnp.dot(per_token, tokens_in, preferred_element_type=jnp.float32).astype(jnp.bfloat16)
    g_send = jnp.dot(
        dispatch, out_grad.reshape(2 * tok_rows, ff_full), preferred_element_type=jnp.float32
    ).astype(jnp.bfloat16)
    valid_slot = jnp.sum(dispatch.astype(jnp.float32), axis=1).astype(jnp.bfloat16)
    send = jnp.concatenate(
        (
            x_send.reshape(group_count, capacity, shard_count, width_dev),
            g_send.reshape(group_count, capacity, shard_count, ff_dev),
            jnp.broadcast_to(
                valid_slot.reshape(group_count, capacity, 1, 1),
                (group_count, capacity, shard_count, MARK),
            ),
        ),
        axis=3,
    )
    send = send.transpose(0, 2, 1, 3).reshape(group_count * shard_count, capacity, -1)
    rows = lax.all_to_all(send, ("expert", "shard"), split_axis=0, concat_axis=0, tiled=True)
    rows = rows.reshape(-1, rows.shape[2])
    own_x = rows[:, :width_dev]
    rows_g = rows[:, width_dev : width_dev + ff_dev]
    row_count = jnp.sum(rows[:, width_dev + ff_dev].astype(jnp.float32)).reshape(1)
    row_total = rows.shape[0]
    rows_x = lax.all_gather(own_x, "shard", axis=0)

    own_blocks = width_dev // BLK
    first_block = lax.axis_index("shard") * own_blocks
    own_levels = lax.dynamic_slice_in_dim(d_levels[0], first_block, own_blocks, 0)
    inv_a = call_blocks(
        input_kernel,
        damping(own_levels),
        row_count,
        own_x,
        jax.ShapeDtypeStruct((own_blocks, BLK, BLK), jnp.float32),
        False,
    )
    inv_a = lax.all_gather(inv_a, "shard", axis=0, tiled=True)
    half = jax.ShapeDtypeStruct((row_total, ff_dev), jnp.bfloat16)
    g_high, g_low = call_blocks(
        hidden_kernel, damping(f_levels[0]), row_count, rows_g, (half, half), True
    )
    blocks = width // BLK
    whole = pl.BlockSpec((row_total, ff_dev), lambda b: (0, 0))
    precond, squares = pl.pallas_call(
        product_kernel,
        grid=(blocks,),
        out_shape=(
            jax.ShapeDtypeStruct((width, ff_dev), jnp.float32),
            jax.ShapeDtypeStruct((8, ff_dev), jnp.float32),
        ),
        in_specs=[
            pl.BlockSpec((1, row_total, BLK), lambda b: (b // own_blocks, 0, b % own_blocks)),
            pl.BlockSpec((1, BLK, BLK), lambda b: (b, 0, 0)),
            whole,
            whole,
        ],
        out_specs=(
            pl.BlockSpec((BLK, ff_dev), lambda b: (b, 0)),
            pl.BlockSpec((8, ff_dev), lambda b: (0, 0)),
        ),
        compiler_params=pltpu.CompilerParams(
            dimension_semantics=("arbitrary",), vmem_limit_bytes=48 << 20
        ),
        cost_estimate=pl.CostEstimate(
            flops=6 * row_total * width * ff_dev, bytes_accessed=4 * width * ff_dev, transcendentals=0
        ),
    )(rows_x, inv_a, g_high, g_low)
    norm_total = lax.psum(jnp.sum(squares), ("expert", "shard"))
    ascent_scale = lax.rsqrt(norm_total / (group_count * width * ff_full) + 1e-06)
    return (precond * ascent_scale).astype(jnp.bfloat16)[None]


class Exchange:
    def __init__(self, group, shards, x_ref, m_ref, xall, rall, sems):
        self.group, self.shards = group, shards
        self.x_ref, self.m_ref, self.xall, self.rall = x_ref, m_ref, xall, rall
        self.zs, self.ys, self.xs, self.ps, self.gs, self.xr, self.gr, self.own = sems
        self.expert = lax.axis_index("expert")
        self.shard = lax.axis_index("shard")
        self.pair = group // 2
        self.depth = shards // self.pair
        self.x, self.core = self.expert // 2, lax.rem(self.expert, 2)
        self.z, self.y = self.shard // self.pair, lax.rem(self.shard, self.pair)
        self.me = self.expert * shards + self.shard
        self.always = self.z >= 0
        self.pending = []
        self.local = []
        self.others = [
            (lax.rem(self.expert + de, group), lax.rem(self.shard + ds, shards))
            for ds in range(shards)
            for de in range(group)
            if de or ds
        ]

    def place(self, x, y, z, core):
        return (x * 2 + core, z * self.pair + y)

    def number(self, x, y, z, core):
        return (x * 2 + core) * self.shards + z * self.pair + y

    def barrier(self):
        barrier = pltpu.get_barrier_semaphore()
        for other in self.others:
            pl.semaphore_signal(barrier, 1, device_id=other, device_id_type=MESH)
        pl.semaphore_wait(barrier, len(self.others))

    def source(self, k, part, unit):
        columns = self.xall.shape[3]
        if k == 0:
            return self.x_ref.at[:, pl.ds(part * columns, columns)]
        return self.xall.at[part, unit]

    def send(self, valid, source, unit, part, target, sem):
        copy = pltpu.make_async_remote_copy(
            src_ref=source,
            dst_ref=self.xall.at[part, unit],
            send_sem=sem,
            recv_sem=self.xr.at[unit * self.xall.shape[0] + part],
            device_id=target,
            device_id_type=MESH,
        )
        pl.when(valid)(copy.start)
        self.pending.append((valid, copy))

    def arrive(self, valid, unit, part):
        @pl.when(valid)
        def _():
            pltpu.make_async_remote_copy(
                src_ref=self.xall.at[part, unit],
                dst_ref=self.xall.at[part, unit],
                send_sem=self.zs.at[0],
                recv_sem=self.xr.at[unit * self.xall.shape[0] + part],
                device_id=(self.expert, self.shard),
                device_id_type=MESH,
            ).wait_recv()

    def sides(self, k):
        if k == 0:
            return [(None, self.always, self.z)]
        return [
            (True, self.z >= k, self.z - k),
            (False, self.z + k <= self.depth - 1, self.z + k),
        ]

    def along(self, k, part):
        parts = self.xall.shape[0]
        for side, valid, origin in self.sides(k):
            unit = self.number(self.x, self.y, origin, self.core)
            if k:
                self.arrive(valid, unit, part)
            for up in (True, False) if side is None else (side,):
                more = jnp.logical_and(valid, self.z < self.depth - 1 if up else self.z > 0)
                target = self.place(self.x, self.y, self.z + (1 if up else -1), self.core)
                sem = self.zs.at[(k * parts + part) * 2 + int(up)]
                self.send(more, self.source(k, part, unit), unit, part, target, sem)

    def beside(self, valid, source, unit, part, axis, sem):
        x, y = (1 - self.x, self.y) if axis == "x" else (self.x, 1 - self.y)
        sems = self.xs if axis == "x" else self.ys
        self.send(valid, source, unit, part, self.place(x, y, self.z, self.core), sems.at[sem])

    def across(self, valid, source, unit, part, sem):
        target = self.place(self.x, self.y, self.z, 1 - self.core)
        self.send(valid, source, unit, part, target, self.ps.at[sem])

    def spread(self, k, part):
        parts = self.xall.shape[0]
        for _, valid, origin in self.sides(k):
            unit = self.number(self.x, self.y, origin, self.core)
            source = self.source(k, part, unit)
            for axis in ("y", "x") if part % 2 == 0 else ("x", "y"):
                self.beside(valid, source, unit, part, axis, origin * parts + part)
            self.across(valid, source, unit, part, origin * parts + part)

    def second(self, k, part):
        parts, depth = self.xall.shape[0], self.depth
        for _, valid, origin in self.sides(k):
            if part % 2 == 0:
                unit, axis = self.number(self.x, 1 - self.y, origin, self.core), "x"
            else:
                unit, axis = self.number(1 - self.x, self.y, origin, self.core), "y"
            self.arrive(valid, unit, part)
            source = self.xall.at[part, unit]
            self.beside(valid, source, unit, part, axis, (depth + origin) * parts + part)
            self.across(valid, source, unit, part, (depth + origin) * parts + part)

    def third(self, k, part):
        parts, depth = self.xall.shape[0], self.depth
        for _, valid, origin in self.sides(k):
            if part % 2 == 0:
                near = self.number(1 - self.x, self.y, origin, self.core)
            else:
                near = self.number(self.x, 1 - self.y, origin, self.core)
            far = self.number(1 - self.x, 1 - self.y, origin, self.core)
            for row, unit in enumerate((near, far)):
                self.arrive(valid, unit, part)
                sem = ((2 + row) * depth + origin) * parts + part
                self.across(valid, self.xall.at[part, unit], unit, part, sem)

    def begin(self, parts):
        for part in parts:
            self.along(0, part)
        for part in parts:
            self.spread(0, part)

    def keep(self):
        columns = self.xall.shape[3]
        for part in range(self.xall.shape[0]):
            source = self.x_ref.at[:, pl.ds(part * columns, columns)]
            self.local.append(pltpu.make_async_copy(source, self.xall.at[part, self.me], self.own.at[part]))
        self.local.append(
            pltpu.make_async_copy(self.m_ref.at[self.me], self.rall.at[self.me], self.own.at[self.xall.shape[0]])
        )
        for copy in self.local:
            copy.start()

    def step(self, k, parts):
        if k < self.depth:
            for part in parts:
                self.along(k, part)
            for part in parts:
                self.spread(k, part)
        if k <= self.depth:
            for part in parts:
                self.second(k - 1, part)
        if k >= 2:
            for part in parts:
                self.third(k - 2, part)

    def finish(self, parts):
        for x in range(2):
            for y in range(self.pair):
                for z in range(self.depth):
                    for part in parts:
                        self.arrive(self.always, self.number(x, y, z, 1 - self.core), part)

    def messages(self, turn, turns):
        for i, other in enumerate(self.others):
            if i % turns != turn:
                continue
            copy = pltpu.make_async_remote_copy(
                src_ref=self.m_ref.at[other[0] * self.shards + other[1]],
                dst_ref=self.rall.at[self.me],
                send_sem=self.gs.at[i],
                recv_sem=self.gr.at[self.me],
                device_id=other,
                device_id_type=MESH,
            )
            copy.start()
            self.pending.append((self.always, copy))

    def wait_messages(self):
        for other in self.others:
            there = other[0] * self.shards + other[1]
            pltpu.make_async_remote_copy(
                src_ref=self.m_ref.at[there],
                dst_ref=self.rall.at[there],
                send_sem=self.gs.at[0],
                recv_sem=self.gr.at[there],
                device_id=(self.expert, self.shard),
                device_id_type=MESH,
            ).wait_recv()

    def drain(self):
        for valid, copy in self.pending:
            pl.when(valid)(copy.wait_send)


def leaf_inverse(work, packs, service):
    _, size, lanes = work.shape
    lane = lax.broadcasted_iota(jnp.int32, (8, lanes), 1)
    inner = lax.rem(lane, size)
    base = lane - inner

    def take(value, index):
        return jnp.take_along_axis(value, index, axis=1)

    def step(i, carry):
        j = i * 2
        at0, at1 = inner == j, inner == j + 1
        index0, index1 = base + j, base + j + 1
        pivot = jnp.logical_or(at0, at1)
        rows = []
        for p in range(packs):
            r0 = jnp.broadcast_to(work[p, pl.ds(j, 1), :], (8, lanes))
            r1 = jnp.broadcast_to(work[p, pl.ds(j + 1, 1), :], (8, lanes))
            a, b = take(r0, index0), take(r0, index1)
            c, d = take(r1, index0), take(r1, index1)
            scale = 1.0 / (a * d - b * c)
            r0 = jnp.where(at0, 1.0, jnp.where(at1, 0.0, r0))
            r1 = jnp.where(at1, 1.0, jnp.where(at0, 0.0, r1))
            rows.append(((d * scale) * r0 - (b * scale) * r1, (a * scale) * r1 - (c * scale) * r0))
        for p in range(packs):
            s0, s1 = rows[p]
            for t in range(0, size, 8):
                m = work[p, t : t + 8, :]
                c0, c1 = take(m, index0), take(m, index1)
                work[p, t : t + 8, :] = jnp.where(pivot, 0.0, m) - c0 * s0 - c1 * s1
        for p in range(packs):
            s0, s1 = rows[p]
            work[p, pl.ds(j, 1), :] = s0[:1]
            work[p, pl.ds(j + 1, 1), :] = s1[:1]
        return carry

    lax.fori_loop(0, size // 4, step, 0)
    service()
    lax.fori_loop(size // 4, size // 2, step, 0)
    service()


def invert(cov, first, count, work, side_ref, mid_ref, service):
    full = cov.shape[1]
    leaf = work.shape[1]
    per = work.shape[2] // leaf

    def solve_leaf(offset):
        span = slice(offset, offset + leaf)
        for p in range(count // per):
            parts = [cov[first + p * per + i, span, span] for i in range(per)]
            work[p] = jnp.concatenate(parts, axis=1)
        leaf_inverse(work, count // per, service)
        for p in range(count // per):
            for i in range(per):
                cov[first + p * per + i, span, span] = work[p][:, i * leaf : (i + 1) * leaf]

    def solve(offset, size):
        if size == leaf:
            solve_leaf(offset)
            return
        half = size // 2
        one, two = slice(offset, offset + half), slice(offset + half, offset + size)
        solve(offset, half)
        store = side_ref if size == full else mid_ref
        for n in range(count):
            m = first + n
            upper = cov[m, one, two]
            side = dot_f32(cov[m, one, one], upper)
            store[n] = side
            cov[m, two, two] = cov[m, two, two] - dot_f32(upper, side, TN)
        solve(offset + half, half)
        for n in range(count):
            m = first + n
            last = cov[m, two, two]
            side = store[n]
            corner = dot_f32(side, last)
            cov[m, one, one] = cov[m, one, one] + dot_f32(corner, side, NT)
            cov[m, one, two] = -corner
            cov[m, two, one] = -corner.T

    solve(0, full)


def same(shape, rows, columns):
    return rows(lax.broadcasted_iota(jnp.int32, shape, 0)) == columns(lax.broadcasted_iota(jnp.int32, shape, 1))


def one_hot(mask):
    return jnp.where(mask, 1.0, 0.0).astype(jnp.bfloat16)


def three(a, b):
    return dot_bf16(a[0], b[1]) + dot_bf16(a[1], b[0]) + dot_bf16(a[0], b[0])


def fused_kernel(
    group,
    shards,
    tokens,
    main,
    entries,
    damp_a,
    damp_f,
    x_ref,
    m_ref,
    out_ref,
    scale_ref,
    xall,
    rall,
    picks,
    xc,
    gc,
    cov,
    work,
    side,
    mid,
    norm,
    parts,
    *sems,
):
    part_send, part_recv = sems[-2:]
    exchange = Exchange(group, shards, x_ref, m_ref, xall, rall, sems[:-2])
    depth = exchange.depth
    exchange.barrier()
    exchange.begin((0, 1))
    exchange.keep()
    for k in range(1, depth + 2):
        exchange.step(k, (0, 1))
        if k <= 3:
            exchange.messages(k - 1, 3)
    exchange.begin((2, 3))
    exchange.finish((0, 1))
    exchange.wait_messages()
    for copy in exchange.local:
        copy.wait()

    steps = list(range(1, depth + 2))

    def service():
        if steps:
            exchange.step(steps.pop(0), (2, 3))

    sources = group * shards
    ff = gc.shape[1]
    blocks = ff // BLK
    extra = main // blocks
    batch = BLK // tokens
    groups = sources // batch
    rows_main, rows_extra = batch * main, batch * extra
    rows_all = rows_main + rows_extra
    columns = xall.shape[3]
    tile_main = one_hot(same((MARK, BLK), lambda i: i, lambda j: lax.rem(j, tokens)))
    tile_extra = one_hot(same((MARK, BLK), lambda i: i - tokens, lambda j: lax.rem(j, tokens)))
    owner = same((rows_main, BLK), lambda i: i // main, lambda j: j // tokens)

    def chosen(shift):
        mask = same((rows_extra, rows_main), lambda i: (i // extra) * main + shift + lax.rem(i, extra), lambda j: j)
        return one_hot(mask)

    total = jnp.zeros((), jnp.float32)
    for g in range(groups):
        part = rall[g * batch : (g + 1) * batch].reshape(rows_main, -1)
        marks = part[:, ff + BLK :]
        pick = jnp.where(owner, dot_bf16(marks, tile_main), 0.0)
        rest = jnp.where(owner, dot_bf16(marks, tile_extra), 0.0).astype(jnp.bfloat16)
        rest = dot_bf16(chosen(0), rest)
        total = total + jnp.sum(pick) + jnp.sum(rest)
        base = g * rows_all
        picks[base : base + rows_main, :] = pick.astype(jnp.bfloat16)
        picks[base + rows_main : base + rows_all, :] = rest.astype(jnp.bfloat16)
        gc[base : base + rows_main, :] = part[:, :ff]
        for q in range(blocks):
            spread = dot_bf16(chosen(q * extra), part[:, ff : ff + BLK])
            gc[base + rows_main : base + rows_all, q * BLK : (q + 1) * BLK] = spread.astype(jnp.bfloat16)

    def select_rows(part):
        for g in range(groups):
            rows = xall[part, g * batch : (g + 1) * batch].reshape(BLK, columns)
            span = slice(g * rows_all, (g + 1) * rows_all)
            xc[span, part * columns : (part + 1) * columns] = dot_bf16(picks[span, :], rows).astype(jnp.bfloat16)

    scale = 1.0 / jnp.broadcast_to(total, (1, 1))
    eye = same((BLK, BLK), lambda i: i, lambda j: j)
    count_a = xc.shape[1] // BLK
    half = count_a // 2

    def covariance(to, rows, damp):
        cov[to] = dot_bf16(rows, rows, TN) * scale + jnp.where(eye, damp, 0.0)

    def slot(b):
        return b + jnp.where(b >= half, blocks, 0)

    select_rows(0)
    select_rows(1)
    for b in range(half):
        covariance(b, xc[:, b * BLK : (b + 1) * BLK], damp_a[b])
    for b in range(blocks):
        covariance(half + b, gc[:, b * BLK : (b + 1) * BLK], damp_f[b])
    service()
    invert(cov, 0, half + blocks, work, side, mid, service)
    while steps:
        service()
    exchange.finish((2, 3))
    select_rows(2)
    select_rows(3)
    for b in range(half, count_a):
        covariance(blocks + b, xc[:, b * BLK : (b + 1) * BLK], damp_a[b])
    invert(cov, half + blocks, half, work, side, mid, service)

    norm[...] = jnp.zeros_like(norm)

    def product(b, carry):
        across = pl.multiple_of(b * BLK, BLK)
        gradient = dot_bf16(xc[:, pl.ds(across, BLK)], gc[...], TN)
        left = split(cov[slot(b)], 2)
        for c in range(blocks):
            right = three(split(gradient[:, c * BLK : (c + 1) * BLK], 2), split(cov[half + c], 2))
            out = three(left, split(right, 2))
            out_ref[pl.ds(across, BLK), c * BLK : (c + 1) * BLK] = out
            norm[...] += jnp.sum((out * out).reshape(-1, 8, BLK), axis=0)
        return carry

    lax.fori_loop(0, count_a, product, 0)
    parts[exchange.me] = norm[:, :MARK] + norm[:, MARK:]
    exchange.drain()
    copies = []
    for i, other in enumerate(exchange.others):
        copy = pltpu.make_async_remote_copy(
            src_ref=parts.at[exchange.me],
            dst_ref=parts.at[exchange.me],
            send_sem=part_send.at[i],
            recv_sem=part_recv.at[exchange.me],
            device_id=other,
            device_id_type=MESH,
        )
        copy.start()
        copies.append(copy)
    for other in exchange.others:
        there = other[0] * shards + other[1]
        pltpu.make_async_remote_copy(
            src_ref=parts.at[there],
            dst_ref=parts.at[there],
            send_sem=part_send.at[0],
            recv_sem=part_recv.at[there],
            device_id=(exchange.expert, exchange.shard),
            device_id_type=MESH,
        ).wait_recv()
    norm_total = jnp.sum(jnp.sum(parts[...], axis=0))
    scale_ref[...] = lax.rsqrt(jnp.broadcast_to(norm_total, scale_ref.shape) * (1.0 / entries) + 1e-06)
    for copy in copies:
        copy.wait_send()


def scale_kernel(value_ref, scale_ref, out_ref, slots, sems):
    depth, rows = slots.shape[:2]
    scale = scale_ref[0:1, 0:1]
    count = value_ref.shape[0] // rows

    def out(i):
        to = pl.multiple_of(i * rows, rows)
        at = lax.rem(i, depth)
        return pltpu.make_async_copy(slots.at[at], out_ref.at[pl.ds(to, rows), :], sems.at[at])

    def step(i, carry):
        @pl.when(i >= depth)
        def _():
            out(i - depth).wait()

        from_row = pl.multiple_of(i * rows, rows)
        slots[lax.rem(i, depth)] = (value_ref[pl.ds(from_row, rows), :] * scale).astype(slots.dtype)
        out(i).start()
        return carry

    lax.fori_loop(0, count, step, 0)
    for i in range(count - depth, count):
        out(i).wait()


def capacity_of(tok_rows, group_count):
    return min(tok_rows, max(2, 5 * tok_rows // (2 * group_count)))


def pack_messages(out_grad, expert_ids, group_count, shard_count, capacity, main):
    tok_rows, _, ff_full = out_grad.shape
    ff_dev = ff_full // shard_count
    extra = capacity - main
    total = group_count * shard_count
    flat_ids = expert_ids.reshape(-1)
    member = (flat_ids[:, None] == jnp.arange(group_count, dtype=jnp.int32)[None, :]).astype(jnp.int32)
    before = jnp.cumsum(member, axis=0) - member
    ranking = jnp.sum(before * member, axis=1)
    target = flat_ids * capacity + ranking
    dispatch = (jnp.arange(group_count * capacity, dtype=jnp.int32)[:, None] == target[None, :]).astype(jnp.bfloat16)
    per_token = jnp.sum(dispatch.reshape(-1, tok_rows, 2).astype(jnp.float32), axis=2).astype(jnp.bfloat16)
    sent = jnp.dot(dispatch, out_grad.reshape(2 * tok_rows, ff_full), preferred_element_type=jnp.float32)
    sent = sent.astype(jnp.bfloat16).reshape(group_count, capacity, ff_full)
    marks = per_token.reshape(group_count, capacity, tok_rows)
    first = sent[:, :main].reshape(group_count, main, shard_count, ff_dev).transpose(0, 2, 1, 3)
    last = sent[:, main:].reshape(group_count, extra, shard_count, ff_dev // BLK, BLK).transpose(0, 2, 3, 1, 4)
    info = jnp.concatenate(
        (
            marks[:, :main],
            jnp.pad(marks[:, main:], ((0, 0), (0, main - extra), (0, 0))),
            jnp.zeros((group_count, main, MARK - 2 * tok_rows), jnp.bfloat16),
        ),
        axis=2,
    )
    return jnp.concatenate(
        (
            first.reshape(total, main, ff_dev),
            last.reshape(total, main, BLK),
            jnp.broadcast_to(info[:, None], (group_count, shard_count, main, MARK)).reshape(total, main, MARK),
        ),
        axis=2,
    )


def fast(tokens_in, out_grad, expert_ids, d_levels, f_levels):
    group_count = lax.axis_size("expert")
    shard_count = lax.axis_size("shard")
    tok_rows, width = tokens_in.shape
    ff_full = out_grad.shape[2]
    ff_dev = ff_full // shard_count
    blocks = ff_dev // BLK
    count_a = width // BLK
    capacity = capacity_of(tok_rows, group_count)
    main = 16 * (capacity // 16)
    total = group_count * shard_count
    depth = shard_count // (group_count // 2)
    messages = pack_messages(out_grad, expert_ids, group_count, shard_count, capacity, main)
    row_total = total * capacity
    count = count_a // 2 + blocks
    vmem = pl.BlockSpec(memory_space=pltpu.VMEM)
    smem = pl.BlockSpec(memory_space=pltpu.SMEM)
    f32, bf16, dma = jnp.float32, jnp.bfloat16, pltpu.SemaphoreType.DMA
    precond, scale = pl.pallas_call(
        functools.partial(fused_kernel, group_count, shard_count, tok_rows, main, group_count * width * ff_full),
        out_shape=(
            pltpu.VMEM((width, ff_dev), f32),
            jax.ShapeDtypeStruct((8, 128), f32),
        ),
        in_specs=[smem, smem, vmem, vmem],
        out_specs=(vmem, vmem),
        scratch_shapes=[
            pltpu.VMEM((4, total, tok_rows, width // 4), bf16),
            pltpu.VMEM(messages.shape, bf16),
            pltpu.VMEM((row_total, BLK), bf16),
            pltpu.VMEM((row_total, width), bf16),
            pltpu.VMEM((row_total, ff_dev), bf16),
            pltpu.VMEM((count_a + blocks, BLK, BLK), f32),
            pltpu.VMEM((count // 2, LEAF, 128), f32),
            pltpu.VMEM((count, HALF, HALF), f32),
            pltpu.VMEM((count, HALF // 2, HALF // 2), f32),
            pltpu.VMEM((8, BLK), f32),
            pltpu.VMEM((total, 8, MARK), f32),
            dma((8 * depth,)),
            dma((8 * depth,)),
            dma((8 * depth,)),
            dma((16 * depth,)),
            dma((total,)),
            dma((4 * total,)),
            dma((total,)),
            dma((5,)),
            dma((total,)),
            dma((total,)),
        ],
        compiler_params=pltpu.CompilerParams(collective_id=0, has_side_effects=True, vmem_limit_bytes=36 << 20),
    )(damping(d_levels[0]), damping(f_levels[0]), tokens_in, messages)
    ascent = pl.pallas_call(
        scale_kernel,
        out_shape=jax.ShapeDtypeStruct((width, ff_dev), bf16),
        in_specs=[vmem, vmem],
        out_specs=pl.BlockSpec(memory_space=pl.ANY),
        scratch_shapes=[pltpu.VMEM((4, BLK, ff_dev), bf16), dma((4,))],
        compiler_params=pltpu.CompilerParams(vmem_limit_bytes=8 << 20),
    )(precond, scale)
    return ascent[None]


def local(tokens_in, out_grad, expert_ids, d_levels, f_levels):
    group_count = lax.axis_size("expert")
    shard_count = lax.axis_size("shard")
    tok_rows, width = tokens_in.shape
    blocks = out_grad.shape[2] // shard_count // BLK
    main = 16 * (capacity_of(tok_rows, group_count) // 16)
    extra = capacity_of(tok_rows, group_count) - main
    chips = group_count // 2 == 2 and shard_count % 2 == 0
    packed = main > 0 and extra * blocks == main and 2 * tok_rows <= MARK and BLK % tok_rows == 0
    even = (group_count * shard_count * tok_rows) % BLK == 0 and width % (4 * BLK) == 0 and blocks % 2 == 0
    small = group_count * shard_count * tok_rows * width * 2 <= 12 << 20
    if chips and packed and even and small:
        return fast(tokens_in, out_grad, expert_ids, d_levels, f_levels)
    return plain(tokens_in, out_grad, expert_ids, d_levels, f_levels)


def solution(mesh):
    return jax.shard_map(
        local,
        mesh=mesh,
        in_specs=(
            P(("expert", "shard"), None),
            P(("expert", "shard"), None, None),
            P(("expert", "shard"), None),
            P("expert", None),
            P("expert", "shard"),
        ),
        out_specs=P("expert", None, "shard"),
        check_vma=False,
    )
```

```python
import functools

import jax
import jax.numpy as jnp
from jax import lax
from jax.experimental import pallas as pl
from jax.experimental.pallas import tpu as pltpu
from jax.sharding import PartitionSpec as P

BLK = 256
HALF = BLK // 2
MARK = 128
LEAF = 32
MESH = pl.DeviceIdType.MESH
NN = (((1,), (0,)), ((), ()))
NT = (((1,), (1,)), ((), ()))
TN = (((0,), (0,)), ((), ()))


def dot_f32(a, b, dims=(((1,), (0,)), ((), ()))):
    return lax.dot_general(
        a, b, dims, precision=lax.Precision.HIGHEST, preferred_element_type=jnp.float32
    )


def dot_bf16(a, b, dims=(((1,), (0,)), ((), ()))):
    return lax.dot_general(a, b, dims, preferred_element_type=jnp.float32)


def split(value, parts):
    out = []
    for _ in range(parts):
        part = value.astype(jnp.bfloat16)
        out.append(part)
        value = value - part.astype(jnp.float32)
    return out


def gauss_jordan(work, count):
    lanes = lax.broadcasted_iota(jnp.int32, (HALF, HALF), 1)
    lane_row = lax.broadcasted_iota(jnp.int32, (1, HALF), 1)

    def step(j, carry):
        index = jnp.full((HALF, HALF), j, jnp.int32)
        at_pivot = lanes == j
        matrices = [work[b] for b in range(count)]
        rows = [work[b, pl.ds(j, 1), :] for b in range(count)]
        pivots = [
            jnp.sum(jnp.where(lane_row == j, row, 0.0), axis=1, keepdims=True) for row in rows
        ]
        columns = [jnp.take_along_axis(matrix, index, axis=1) for matrix in matrices]
        scaled = [
            jnp.where(lane_row == j, 1.0, row) / pivot for row, pivot in zip(rows, pivots)
        ]
        updated = [
            jnp.where(at_pivot, 0.0, matrix) - column * row
            for matrix, column, row in zip(matrices, columns, scaled)
        ]
        for b in range(count):
            work[b] = updated[b]
        for b in range(count):
            work[b, pl.ds(j, 1), :] = scaled[b]
        return carry

    lax.fori_loop(0, HALF, step, 0)


def invert_covariances(rows_ref, damp_ref, count_ref, work, cov, aux):
    count = cov.shape[0]
    eye = (
        lax.broadcasted_iota(jnp.int32, (BLK, BLK), 0)
        == lax.broadcasted_iota(jnp.int32, (BLK, BLK), 1)
    )
    for b in range(count):
        rows = rows_ref[:, b * BLK : (b + 1) * BLK]
        product = dot_bf16(rows, rows, TN) / count_ref[0]
        cov[b] = product + jnp.where(eye, damp_ref[b], 0.0)
        work[b] = cov[b, :HALF, :HALF]
    gauss_jordan(work, count)
    for b in range(count):
        first = work[b]
        upper = cov[b, :HALF, HALF:]
        side = dot_f32(first, upper)
        aux[b] = side
        cov[b, :HALF, :HALF] = first
        work[b] = cov[b, HALF:, HALF:] - dot_f32(upper, side, TN)
    gauss_jordan(work, count)
    for b in range(count):
        last = work[b]
        side = aux[b]
        corner = dot_f32(side, last)
        cov[b, :HALF, :HALF] = cov[b, :HALF, :HALF] + dot_f32(corner, side, NT)
        cov[b, :HALF, HALF:] = -corner
        cov[b, HALF:, :HALF] = -corner.T
        cov[b, HALF:, HALF:] = last


def input_kernel(damp_ref, count_ref, rows_ref, inv_ref, work, aux):
    invert_covariances(rows_ref, damp_ref, count_ref, work, inv_ref, aux)


def hidden_kernel(damp_ref, count_ref, rows_ref, high_ref, low_ref, work, aux, cov):
    invert_covariances(rows_ref, damp_ref, count_ref, work, cov, aux)
    for b in range(cov.shape[0]):
        columns = slice(b * BLK, (b + 1) * BLK)
        rows = rows_ref[:, columns]
        total = sum(dot_bf16(rows, part) for part in reversed(split(cov[b], 3)))
        high_ref[:, columns], low_ref[:, columns] = split(total, 2)


def product_kernel(rows_ref, inv_ref, high_ref, low_ref, out_ref, norm_ref):
    rows = rows_ref[0]
    left = sum(dot_bf16(part, rows, NT) for part in reversed(split(inv_ref[0], 3)))
    left_high, left_low = split(left, 2)
    high = high_ref[...]
    out = dot_bf16(left_high, low_ref[...]) + dot_bf16(left_low, high) + dot_bf16(left_high, high)
    out_ref[...] = out

    @pl.when(pl.program_id(0) == 0)
    def _():
        norm_ref[...] = jnp.zeros_like(norm_ref)

    norm_ref[...] += jnp.sum((out * out).reshape(-1, 8, out.shape[1]), axis=0)


def damping(levels):
    return 0.05 * jnp.exp(0.4 * levels.astype(jnp.float32))


def call_blocks(kernel, damp, row_count, rows, out_shape, with_cov):
    count = damp.shape[0]
    scratch = [pltpu.VMEM((count, HALF, HALF), jnp.float32)] * 2
    if with_cov:
        scratch.append(pltpu.VMEM((count, BLK, BLK), jnp.float32))
    vmem = pl.BlockSpec(memory_space=pltpu.VMEM)
    smem = pl.BlockSpec(memory_space=pltpu.SMEM)
    return pl.pallas_call(
        kernel,
        out_shape=out_shape,
        in_specs=[smem, smem, vmem],
        out_specs=jax.tree.map(lambda _: vmem, out_shape),
        scratch_shapes=scratch,
        compiler_params=pltpu.CompilerParams(vmem_limit_bytes=48 << 20),
        cost_estimate=pl.CostEstimate(flops=20_000_000_000, bytes_accessed=4_000_000, transcendentals=0),
    )(damp, row_count, rows)


def plain(tokens_in, out_grad, expert_ids, d_levels, f_levels):
    group_count = lax.axis_size("expert")
    shard_count = lax.axis_size("shard")
    tok_rows = tokens_in.shape[0]
    width = tokens_in.shape[1]
    ff_full = out_grad.shape[2]
    ff_dev = ff_full // shard_count
    width_dev = width // shard_count
    capacity = min(tok_rows, max(2, 5 * tok_rows // (2 * group_count)))
    slot_total = group_count * capacity
    flat_ids = expert_ids.reshape(-1)
    member = (flat_ids[:, None] == jnp.arange(group_count, dtype=jnp.int32)[None, :]).astype(
        jnp.int32
    )
    before = jnp.cumsum(member, axis=0) - member
    ranking = jnp.sum(before * member, axis=1)
    target = flat_ids * capacity + ranking
    dispatch = (jnp.arange(slot_total, dtype=jnp.int32)[:, None] == target[None, :]).astype(
        jnp.bfloat16
    )
    per_token = jnp.sum(
        dispatch.reshape(slot_total, tok_rows, 2).astype(jnp.float32), axis=2
    ).astype(jnp.bfloat16)
    x_send = jnp.dot(per_token, tokens_in, preferred_element_type=jnp.float32).astype(jnp.bfloat16)
    g_send = jnp.dot(
        dispatch, out_grad.reshape(2 * tok_rows, ff_full), preferred_element_type=jnp.float32
    ).astype(jnp.bfloat16)
    valid_slot = jnp.sum(dispatch.astype(jnp.float32), axis=1).astype(jnp.bfloat16)
    send = jnp.concatenate(
        (
            x_send.reshape(group_count, capacity, shard_count, width_dev),
            g_send.reshape(group_count, capacity, shard_count, ff_dev),
            jnp.broadcast_to(
                valid_slot.reshape(group_count, capacity, 1, 1),
                (group_count, capacity, shard_count, MARK),
            ),
        ),
        axis=3,
    )
    send = send.transpose(0, 2, 1, 3).reshape(group_count * shard_count, capacity, -1)
    rows = lax.all_to_all(send, ("expert", "shard"), split_axis=0, concat_axis=0, tiled=True)
    rows = rows.reshape(-1, rows.shape[2])
    own_x = rows[:, :width_dev]
    rows_g = rows[:, width_dev : width_dev + ff_dev]
    row_count = jnp.sum(rows[:, width_dev + ff_dev].astype(jnp.float32)).reshape(1)
    row_total = rows.shape[0]
    rows_x = lax.all_gather(own_x, "shard", axis=0)

    own_blocks = width_dev // BLK
    first_block = lax.axis_index("shard") * own_blocks
    own_levels = lax.dynamic_slice_in_dim(d_levels[0], first_block, own_blocks, 0)
    inv_a = call_blocks(
        input_kernel,
        damping(own_levels),
        row_count,
        own_x,
        jax.ShapeDtypeStruct((own_blocks, BLK, BLK), jnp.float32),
        False,
    )
    inv_a = lax.all_gather(inv_a, "shard", axis=0, tiled=True)
    half = jax.ShapeDtypeStruct((row_total, ff_dev), jnp.bfloat16)
    g_high, g_low = call_blocks(
        hidden_kernel, damping(f_levels[0]), row_count, rows_g, (half, half), True
    )
    blocks = width // BLK
    whole = pl.BlockSpec((row_total, ff_dev), lambda b: (0, 0))
    precond, squares = pl.pallas_call(
        product_kernel,
        grid=(blocks,),
        out_shape=(
            jax.ShapeDtypeStruct((width, ff_dev), jnp.float32),
            jax.ShapeDtypeStruct((8, ff_dev), jnp.float32),
        ),
        in_specs=[
            pl.BlockSpec((1, row_total, BLK), lambda b: (b // own_blocks, 0, b % own_blocks)),
            pl.BlockSpec((1, BLK, BLK), lambda b: (b, 0, 0)),
            whole,
            whole,
        ],
        out_specs=(
            pl.BlockSpec((BLK, ff_dev), lambda b: (b, 0)),
            pl.BlockSpec((8, ff_dev), lambda b: (0, 0)),
        ),
        compiler_params=pltpu.CompilerParams(
            dimension_semantics=("arbitrary",), vmem_limit_bytes=48 << 20
        ),
        cost_estimate=pl.CostEstimate(
            flops=6 * row_total * width * ff_dev, bytes_accessed=4 * width * ff_dev, transcendentals=0
        ),
    )(rows_x, inv_a, g_high, g_low)
    norm_total = lax.psum(jnp.sum(squares), ("expert", "shard"))
    ascent_scale = lax.rsqrt(norm_total / (group_count * width * ff_full) + 1e-06)
    return (precond * ascent_scale).astype(jnp.bfloat16)[None]


class Exchange:
    def __init__(self, group, shards, x_ref, m_ref, info_ref, xall, rall, iall, sems):
        self.group, self.shards = group, shards
        self.x_ref, self.m_ref, self.info_ref = x_ref, m_ref, info_ref
        self.xall, self.rall, self.iall = xall, rall, iall
        self.zs, self.ys, self.xs, self.ps, self.gs, self.xr, self.gr, self.own, self.ns, self.nr = sems
        self.expert = lax.axis_index("expert")
        self.shard = lax.axis_index("shard")
        self.pair = group // 2
        self.depth = shards // self.pair
        self.x, self.core = self.expert // 2, lax.rem(self.expert, 2)
        self.z, self.y = self.shard // self.pair, lax.rem(self.shard, self.pair)
        self.me = self.expert * shards + self.shard
        self.always = self.z >= 0
        self.pending = []
        self.local = []
        self.others = [
            (lax.rem(self.expert + de, group), lax.rem(self.shard + ds, shards))
            for ds in range(shards)
            for de in range(group)
            if de or ds
        ]

    def place(self, x, y, z, core):
        return (x * 2 + core, z * self.pair + y)

    def number(self, x, y, z, core):
        return (x * 2 + core) * self.shards + z * self.pair + y

    def barrier(self):
        barrier = pltpu.get_barrier_semaphore()
        for other in self.others:
            pl.semaphore_signal(barrier, 1, device_id=other, device_id_type=MESH)
        pl.semaphore_wait(barrier, len(self.others))

    def source(self, k, part, unit):
        columns = self.xall.shape[3]
        if k == 0:
            return self.x_ref.at[:, pl.ds(part * columns, columns)]
        return self.xall.at[part, unit]

    def send(self, valid, source, unit, part, target, sem):
        copy = pltpu.make_async_remote_copy(
            src_ref=source,
            dst_ref=self.xall.at[part, unit],
            send_sem=sem,
            recv_sem=self.xr.at[unit * self.xall.shape[0] + part],
            device_id=target,
            device_id_type=MESH,
        )
        pl.when(valid)(copy.start)
        self.pending.append((valid, copy))

    def arrive(self, valid, unit, part):
        @pl.when(valid)
        def _():
            pltpu.make_async_remote_copy(
                src_ref=self.xall.at[part, unit],
                dst_ref=self.xall.at[part, unit],
                send_sem=self.zs.at[0],
                recv_sem=self.xr.at[unit * self.xall.shape[0] + part],
                device_id=(self.expert, self.shard),
                device_id_type=MESH,
            ).wait_recv()

    def sides(self, k):
        if k == 0:
            return [(None, self.always, self.z)]
        return [
            (True, self.z >= k, self.z - k),
            (False, self.z + k <= self.depth - 1, self.z + k),
        ]

    def along(self, k, part):
        parts = self.xall.shape[0]
        for side, valid, origin in self.sides(k):
            unit = self.number(self.x, self.y, origin, self.core)
            if k:
                self.arrive(valid, unit, part)
            for up in (True, False) if side is None else (side,):
                more = jnp.logical_and(valid, self.z < self.depth - 1 if up else self.z > 0)
                target = self.place(self.x, self.y, self.z + (1 if up else -1), self.core)
                sem = self.zs.at[(k * parts + part) * 2 + int(up)]
                self.send(more, self.source(k, part, unit), unit, part, target, sem)

    def beside(self, valid, source, unit, part, axis, sem):
        x, y = (1 - self.x, self.y) if axis == "x" else (self.x, 1 - self.y)
        sems = self.xs if axis == "x" else self.ys
        self.send(valid, source, unit, part, self.place(x, y, self.z, self.core), sems.at[sem])

    def across(self, valid, source, unit, part, sem):
        target = self.place(self.x, self.y, self.z, 1 - self.core)
        self.send(valid, source, unit, part, target, self.ps.at[sem])

    def spread(self, k, part):
        parts = self.xall.shape[0]
        for _, valid, origin in self.sides(k):
            unit = self.number(self.x, self.y, origin, self.core)
            source = self.source(k, part, unit)
            for axis in ("y", "x") if part % 2 == 0 else ("x", "y"):
                self.beside(valid, source, unit, part, axis, origin * parts + part)
            self.across(valid, source, unit, part, origin * parts + part)

    def second(self, k, part):
        parts, depth = self.xall.shape[0], self.depth
        for _, valid, origin in self.sides(k):
            if part % 2 == 0:
                unit, axis = self.number(self.x, 1 - self.y, origin, self.core), "x"
            else:
                unit, axis = self.number(1 - self.x, self.y, origin, self.core), "y"
            self.arrive(valid, unit, part)
            source = self.xall.at[part, unit]
            self.beside(valid, source, unit, part, axis, (depth + origin) * parts + part)
            self.across(valid, source, unit, part, (depth + origin) * parts + part)

    def third(self, k, part):
        parts, depth = self.xall.shape[0], self.depth
        for _, valid, origin in self.sides(k):
            if part % 2 == 0:
                near = self.number(1 - self.x, self.y, origin, self.core)
            else:
                near = self.number(self.x, 1 - self.y, origin, self.core)
            far = self.number(1 - self.x, 1 - self.y, origin, self.core)
            for row, unit in enumerate((near, far)):
                self.arrive(valid, unit, part)
                sem = ((2 + row) * depth + origin) * parts + part
                self.across(valid, self.xall.at[part, unit], unit, part, sem)

    def begin(self, parts):
        for part in parts:
            self.along(0, part)
        for part in parts:
            self.spread(0, part)

    def keep(self):
        columns = self.xall.shape[3]
        for part in range(self.xall.shape[0]):
            source = self.x_ref.at[:, pl.ds(part * columns, columns)]
            self.local.append(pltpu.make_async_copy(source, self.xall.at[part, self.me], self.own.at[part]))
        self.local.append(
            pltpu.make_async_copy(self.m_ref.at[self.me], self.rall.at[self.me], self.own.at[self.xall.shape[0]])
        )
        self.local.append(
            pltpu.make_async_copy(
                self.info_ref.at[self.expert], self.iall.at[self.me], self.own.at[self.xall.shape[0] + 1]
            )
        )
        for copy in self.local:
            copy.start()

    def inform(self):
        for i, other in enumerate(self.others):
            copy = pltpu.make_async_remote_copy(
                src_ref=self.info_ref.at[other[0]],
                dst_ref=self.iall.at[self.me],
                send_sem=self.ns.at[i],
                recv_sem=self.nr.at[self.me],
                device_id=other,
                device_id_type=MESH,
            )
            copy.start()
            self.pending.append((self.always, copy))

    def wait_info(self):
        for other in self.others:
            there = other[0] * self.shards + other[1]
            pltpu.make_async_remote_copy(
                src_ref=self.iall.at[there],
                dst_ref=self.iall.at[there],
                send_sem=self.ns.at[0],
                recv_sem=self.nr.at[there],
                device_id=(self.expert, self.shard),
                device_id_type=MESH,
            ).wait_recv()

    def relay(self, k, parts):
        for part in parts:
            self.along(k, part)
        for part in parts:
            self.spread(k, part)

    def step(self, k, parts):
        if k < self.depth:
            self.relay(k, parts)
        if k <= self.depth:
            for part in parts:
                self.second(k - 1, part)
        if k >= 2:
            for part in parts:
                self.third(k - 2, part)

    def finish(self, parts):
        for x in range(2):
            for y in range(self.pair):
                for z in range(self.depth):
                    for part in parts:
                        self.arrive(self.always, self.number(x, y, z, 1 - self.core), part)

    def messages(self, turn, turns):
        for i, other in enumerate(self.others):
            if i % turns != turn:
                continue
            copy = pltpu.make_async_remote_copy(
                src_ref=self.m_ref.at[other[0] * self.shards + other[1]],
                dst_ref=self.rall.at[self.me],
                send_sem=self.gs.at[i],
                recv_sem=self.gr.at[self.me],
                device_id=other,
                device_id_type=MESH,
            )
            copy.start()
            self.pending.append((self.always, copy))

    def wait_messages(self):
        for other in self.others:
            there = other[0] * self.shards + other[1]
            pltpu.make_async_remote_copy(
                src_ref=self.m_ref.at[there],
                dst_ref=self.rall.at[there],
                send_sem=self.gs.at[0],
                recv_sem=self.gr.at[there],
                device_id=(self.expert, self.shard),
                device_id_type=MESH,
            ).wait_recv()

    def drain(self):
        for valid, copy in self.pending:
            pl.when(valid)(copy.wait_send)


def leaf_inverse(work, packs, service):
    _, size, lanes = work.shape
    lane = lax.broadcasted_iota(jnp.int32, (8, lanes), 1)
    inner = lax.rem(lane, size)
    base = lane - inner

    def take(value, index):
        return jnp.take_along_axis(value, index, axis=1)

    def step(i, carry):
        j = i * 2
        at0, at1 = inner == j, inner == j + 1
        index0, index1 = base + j, base + j + 1
        pivot = jnp.logical_or(at0, at1)
        rows = []
        for p in range(packs):
            r0 = jnp.broadcast_to(work[p, pl.ds(j, 1), :], (8, lanes))
            r1 = jnp.broadcast_to(work[p, pl.ds(j + 1, 1), :], (8, lanes))
            a, b = take(r0, index0), take(r0, index1)
            c, d = take(r1, index0), take(r1, index1)
            scale = 1.0 / (a * d - b * c)
            r0 = jnp.where(at0, 1.0, jnp.where(at1, 0.0, r0))
            r1 = jnp.where(at1, 1.0, jnp.where(at0, 0.0, r1))
            rows.append(((d * scale) * r0 - (b * scale) * r1, (a * scale) * r1 - (c * scale) * r0))
        for p in range(packs):
            s0, s1 = rows[p]
            for t in range(0, size, 8):
                m = work[p, t : t + 8, :]
                c0, c1 = take(m, index0), take(m, index1)
                work[p, t : t + 8, :] = jnp.where(pivot, 0.0, m) - c0 * s0 - c1 * s1
        for p in range(packs):
            s0, s1 = rows[p]
            work[p, pl.ds(j, 1), :] = s0[:1]
            work[p, pl.ds(j + 1, 1), :] = s1[:1]
        return carry

    lax.fori_loop(0, size // 2, step, 0)
    if service is not None:
        service()


def invert(cov, first, count, work, tops, sides, quarter, side_ref, mid_ref, service):
    full = cov.shape[1]
    half = full // 2
    leaf, lanes = work.shape[1:]
    per = lanes // leaf
    packs = count // per
    diagonal = same((lanes, lanes), lambda i: i // leaf, lambda j: j // leaf)
    group = lax.broadcasted_iota(jnp.int32, (leaf, lanes), 1) // leaf

    def gather(p, rows, columns):
        return jnp.concatenate([quarter[p * per + i, rows, columns] for i in range(per)], axis=1)

    def scatter(p, rows, columns, value):
        for i in range(per):
            quarter[p * per + i, rows, columns] = value[:, i * leaf : (i + 1) * leaf]

    def spread(value):
        return jnp.where(diagonal, jnp.concatenate([value] * per, axis=0), 0.0)

    def fold(value):
        out = jnp.where(group == 0, value[:leaf], 0.0)
        for i in range(1, per):
            out = jnp.where(group == i, value[i * leaf : (i + 1) * leaf], out)
        return out

    def solve_pair(offset):
        one, two = slice(offset, offset + leaf), slice(offset + leaf, offset + 2 * leaf)
        for p in range(packs):
            work[p] = gather(p, one, one)
        leaf_inverse(work, packs, service)
        for p in range(packs):
            top = work[p]
            upper = gather(p, one, two)
            side = dot_f32(top, spread(upper))
            tops[p] = top
            sides[p] = side
            work[p] = gather(p, two, two) - fold(dot_f32(upper, side, TN))
        leaf_inverse(work, packs, service)
        for p in range(packs):
            last = work[p]
            side = sides[p]
            wide = spread(side)
            corner = dot_f32(side, spread(last))
            scatter(p, one, one, tops[p] + dot_f32(corner, wide, NT))
            scatter(p, one, two, -corner)
            scatter(p, two, one, -dot_f32(last, wide, NT))
            scatter(p, two, two, last)

    def solve_quarter():
        one, two = slice(0, half // 2), slice(half // 2, half)
        solve_pair(0)
        for n in range(count):
            upper = quarter[n, one, two]
            side = dot_f32(quarter[n, one, one], upper)
            mid_ref[n] = side
            quarter[n, two, two] = quarter[n, two, two] - dot_f32(upper, side, TN)
        solve_pair(half // 2)
        for n in range(count):
            last = quarter[n, two, two]
            side = mid_ref[n]
            corner = dot_f32(side, last)
            quarter[n, one, one] = quarter[n, one, one] + dot_f32(corner, side, NT)
            quarter[n, one, two] = -corner
            quarter[n, two, one] = -corner.T

    one, two = slice(0, half), slice(half, full)

    def between():
        for n in range(count):
            m = first + n
            upper = cov[m, one, two]
            top = quarter[n]
            side = dot_f32(top, upper)
            cov[m, one, one] = top
            side_ref[n] = side
            quarter[n] = cov[m, two, two] - dot_f32(upper, side, TN)

    for n in range(count):
        quarter[n] = cov[first + n, one, one]
    if service is None:

        def turn(h, carry):
            solve_quarter()
            pl.when(h == 0)(between)
            return carry

        lax.fori_loop(0, 2, turn, 0)
    else:
        solve_quarter()
        between()
        solve_quarter()
    for n in range(count):
        m = first + n
        last = quarter[n]
        side = side_ref[n]
        corner = dot_f32(side, last)
        cov[m, one, one] = cov[m, one, one] + dot_f32(corner, side, NT)
        cov[m, one, two] = -corner
        cov[m, two, one] = -corner.T
        cov[m, two, two] = last


def same(shape, rows, columns):
    return rows(lax.broadcasted_iota(jnp.int32, shape, 0)) == columns(lax.broadcasted_iota(jnp.int32, shape, 1))


def one_hot(mask):
    return jnp.where(mask, 1.0, 0.0).astype(jnp.bfloat16)


def three(a, b):
    return dot_bf16(a[0], b[1]) + dot_bf16(a[1], b[0]) + dot_bf16(a[0], b[0])


def pack_rows(group, shards, main, extra, tokens, ids_ref, g_ref, m_ref, info_ref):
    slots = main + extra
    pairs = ids_ref.shape[1]
    ff = m_ref.shape[2] - BLK
    blocks = ff // BLK
    tall = info_ref.shape[1]
    cut = MARK // tokens
    ids = jnp.broadcast_to(ids_ref[...], (8, pairs))
    expert = lax.broadcasted_iota(jnp.int32, (8, pairs), 0)
    member = ids == expert
    earlier = one_hot(lax.broadcasted_iota(jnp.int32, (pairs, pairs), 0) < lax.broadcasted_iota(jnp.int32, (pairs, pairs), 1))
    rank = dot_bf16(one_hot(member), earlier)
    rank = jnp.sum(jnp.where(member, rank, 0.0), axis=0, keepdims=True)
    target = ids_ref[...] * slots + rank.astype(jnp.int32)

    def matches(rows, wanted):
        return wanted(lax.broadcasted_iota(jnp.int32, (rows, pairs), 0)) == target

    pick = one_hot(matches(group * main, lambda i: (i // main) * slots + lax.rem(i, main)))
    rest = matches(group * main, lambda i: (i // main) * slots + main + lax.rem(i, extra))
    turn = lax.broadcasted_iota(jnp.int32, (group * main, pairs), 0) // extra
    rest = jnp.concatenate(
        [one_hot(jnp.logical_and(rest, lax.rem(turn, blocks) == q)) for q in range(blocks)], axis=1
    )
    for s in range(shards):
        rows = g_ref[:, s * ff : (s + 1) * ff]
        first = dot_bf16(pick, rows).astype(jnp.bfloat16)
        tallest = jnp.concatenate([rows[:, q * BLK : (q + 1) * BLK] for q in range(blocks)], axis=0)
        last = dot_bf16(rest, tallest).astype(jnp.bfloat16)
        for e in range(group):
            m_ref[e * shards + s, :, :ff] = first[e * main : (e + 1) * main]
            m_ref[e * shards + s, :, ff:] = last[e * main : (e + 1) * main]
    every = one_hot(matches(group * slots, lambda i: i))
    own = one_hot(same((pairs, MARK), lambda i: i // 2, lambda j: lax.rem(j, tokens)))
    marks = jnp.where(
        same((group * slots, MARK), lambda i: lax.rem(lax.rem(i, slots), cut), lambda j: j // tokens),
        dot_bf16(every, own),
        0.0,
    ).astype(jnp.bfloat16)
    lift = one_hot(
        same(
            (group * tall, group * slots),
            lambda i: i,
            lambda j: (j // slots) * tall + lax.rem(j, slots) // cut,
        )
    )
    info = dot_bf16(lift, marks).astype(jnp.bfloat16)
    for e in range(group):
        info_ref[e] = info[e * tall : (e + 1) * tall]


def fused_kernel(
    group,
    shards,
    tokens,
    main,
    entries,
    level_a,
    level_f,
    x_ref,
    g_ref,
    ids_ref,
    out_ref,
    scale_ref,
    m_ref,
    info_ref,
    xall,
    rall,
    iall,
    picks,
    xc,
    gc,
    cov,
    work,
    tops,
    sides,
    quarter,
    side,
    mid,
    norm,
    parts,
    *sems,
):
    part_send, part_recv = sems[-2:]
    exchange = Exchange(group, shards, x_ref, m_ref, info_ref, xall, rall, iall, sems[:-2])
    depth = exchange.depth
    turns = 4
    sources = group * shards
    ff = gc.shape[1]
    blocks = ff // BLK
    extra = main // blocks
    exchange.barrier()
    exchange.begin((0, 1))
    pack_rows(group, shards, main, extra, tokens, ids_ref, g_ref, m_ref, info_ref)
    for k in range(1, depth + 2):
        exchange.step(k, (0, 1))
        if k == 1:
            exchange.inform()
            exchange.keep()
        if k == depth - 1:
            exchange.begin((2, 3))
        if k == depth:
            exchange.messages(0, turns)
    exchange.wait_info()
    for copy in exchange.local:
        copy.wait()

    late = (2, 3)
    steps = []
    for k in range(1, max(depth, turns)):
        if k < depth:
            steps.append(functools.partial(exchange.relay, k, late))
        if k < turns:
            steps.append(functools.partial(exchange.messages, k, turns))

    def service():
        if steps:
            steps.pop(0)()

    batch = BLK // tokens
    groups = sources // batch
    rows_main, rows_extra = batch * main, batch * extra
    rows_all = rows_main + rows_extra
    columns = xall.shape[3]
    tall = iall.shape[1]
    cut = MARK // tokens

    def source_of(i):
        return jnp.where(i < rows_main, i // main, (i - rows_main) // extra)

    def slot_of(i):
        return jnp.where(i < rows_main, lax.rem(i, main), main + lax.rem(i - rows_main, extra))

    rise = one_hot(same((rows_all, batch * tall), lambda i: source_of(i) * tall + slot_of(i) // cut, lambda j: j))
    inside = same((rows_all, MARK), lambda i: lax.rem(slot_of(i), cut), lambda j: j // tokens)
    tile = one_hot(same((MARK, BLK), lambda i: lax.rem(i, tokens), lambda j: lax.rem(j, tokens)))
    owner = same((rows_all, BLK), source_of, lambda j: j // tokens)
    total = jnp.zeros((), jnp.float32)
    for g in range(groups):
        marks = iall[g * batch : (g + 1) * batch].reshape(batch * tall, MARK)
        marks = jnp.where(inside, dot_bf16(rise, marks), 0.0).astype(jnp.bfloat16)
        pick = jnp.where(owner, dot_bf16(marks, tile), 0.0)
        total = total + jnp.sum(pick)
        picks[g * rows_all : (g + 1) * rows_all, :] = pick.astype(jnp.bfloat16)

    def select_rows(part):
        for g in range(groups):
            rows = xall[part, g * batch : (g + 1) * batch].reshape(BLK, columns)
            span = slice(g * rows_all, (g + 1) * rows_all)
            xc[span, part * columns : (part + 1) * columns] = dot_bf16(picks[span, :], rows).astype(jnp.bfloat16)

    scale = 1.0 / jnp.broadcast_to(total, (1, 1))
    eye = same((BLK, BLK), lambda i: i, lambda j: j)
    count_a = xc.shape[1] // BLK
    half = count_a // 2

    def covariance(to, rows, level):
        damp = 0.05 * jnp.exp(jnp.broadcast_to(0.4 * level.astype(jnp.float32), (1, BLK)))
        cov[to] = dot_bf16(rows, rows, TN) * scale + jnp.where(eye, damp, 0.0)

    def inverses(first, count, service):
        invert(cov, first, count, work, tops, sides, quarter, side, mid, service)

    def gradient(b, carry):
        across = pl.multiple_of(b * BLK, BLK)
        out_ref[pl.ds(across, BLK), :] = dot_bf16(xc[:, pl.ds(across, BLK)], gc[...], TN)
        return carry

    exchange.finish((0, 1))
    select_rows(0)
    select_rows(1)
    for b in range(half):
        covariance(b, xc[:, b * BLK : (b + 1) * BLK], level_a[b])
    inverses(0, half, service)
    while steps:
        service()
    for k in range(depth):
        for part in late:
            exchange.second(k, part)
    exchange.wait_messages()
    for g in range(groups):
        part = rall[g * batch : (g + 1) * batch].reshape(rows_main, -1)
        base = g * rows_all
        gc[base : base + rows_main, :] = part[:, :ff]
        for q in range(blocks):
            chosen = one_hot(
                same((rows_extra, rows_main), lambda i: (i // extra) * main + q * extra + lax.rem(i, extra), lambda j: j)
            )
            moved = dot_bf16(chosen, part[:, ff : ff + BLK])
            gc[base + rows_main : base + rows_all, q * BLK : (q + 1) * BLK] = moved.astype(jnp.bfloat16)
    for b in range(blocks):
        covariance(count_a + b, gc[:, b * BLK : (b + 1) * BLK], level_f[b])
    for k in range(depth):
        for part in late:
            exchange.third(k, part)
    lax.fori_loop(0, half, gradient, 0)
    exchange.finish(late)
    select_rows(2)
    select_rows(3)
    for b in range(half, count_a):
        covariance(b, xc[:, b * BLK : (b + 1) * BLK], level_a[b])
    inverses(half, half + blocks, None)
    lax.fori_loop(half, count_a, gradient, 0)

    norm[...] = jnp.zeros_like(norm)

    def product(b, carry):
        across = pl.multiple_of(b * BLK, BLK)
        left = split(cov[b], 2)
        for c in range(blocks):
            right = three(split(out_ref[pl.ds(across, BLK), c * BLK : (c + 1) * BLK], 2), split(cov[count_a + c], 2))
            out = three(left, split(right, 2))
            out_ref[pl.ds(across, BLK), c * BLK : (c + 1) * BLK] = out
            norm[...] += jnp.sum((out * out).reshape(-1, 8, BLK), axis=0)
        return carry

    lax.fori_loop(0, count_a, product, 0)
    parts[exchange.me] = norm[:, :MARK] + norm[:, MARK:]
    exchange.drain()
    copies = []
    for i, other in enumerate(exchange.others):
        copy = pltpu.make_async_remote_copy(
            src_ref=parts.at[exchange.me],
            dst_ref=parts.at[exchange.me],
            send_sem=part_send.at[i],
            recv_sem=part_recv.at[exchange.me],
            device_id=other,
            device_id_type=MESH,
        )
        copy.start()
        copies.append(copy)
    for other in exchange.others:
        there = other[0] * shards + other[1]
        pltpu.make_async_remote_copy(
            src_ref=parts.at[there],
            dst_ref=parts.at[there],
            send_sem=part_send.at[0],
            recv_sem=part_recv.at[there],
            device_id=(exchange.expert, exchange.shard),
            device_id_type=MESH,
        ).wait_recv()
    norm_total = jnp.sum(jnp.sum(parts[...], axis=0))
    scale_ref[...] = lax.rsqrt(jnp.broadcast_to(norm_total, scale_ref.shape) * (1.0 / entries) + 1e-06)
    for copy in copies:
        copy.wait_send()


def scale_kernel(value_ref, scale_ref, out_ref, slots, sems):
    depth, rows = slots.shape[:2]
    scale = scale_ref[0:1, 0:1]
    count = value_ref.shape[0] // rows

    def out(i):
        to = pl.multiple_of(i * rows, rows)
        at = lax.rem(i, depth)
        return pltpu.make_async_copy(slots.at[at], out_ref.at[pl.ds(to, rows), :], sems.at[at])

    def step(i, carry):
        @pl.when(i >= depth)
        def _():
            out(i - depth).wait()

        from_row = pl.multiple_of(i * rows, rows)
        slots[lax.rem(i, depth)] = (value_ref[pl.ds(from_row, rows), :] * scale).astype(slots.dtype)
        out(i).start()
        return carry

    lax.fori_loop(0, count, step, 0)
    for i in range(count - depth, count):
        out(i).wait()


def capacity_of(tok_rows, group_count):
    return min(tok_rows, max(2, 5 * tok_rows // (2 * group_count)))


def fast(tokens_in, out_grad, expert_ids, d_levels, f_levels):
    group_count = lax.axis_size("expert")
    shard_count = lax.axis_size("shard")
    tok_rows, width = tokens_in.shape
    ff_full = out_grad.shape[2]
    ff_dev = ff_full // shard_count
    blocks = ff_dev // BLK
    count_a = width // BLK
    capacity = capacity_of(tok_rows, group_count)
    main = 16 * (capacity // 16)
    total = group_count * shard_count
    depth = shard_count // (group_count // 2)
    tall = capacity * tok_rows // MARK
    tall += -tall % 8
    row_total = total * capacity
    count = count_a // 2 + blocks
    vmem = pl.BlockSpec(memory_space=pltpu.VMEM)
    smem = pl.BlockSpec(memory_space=pltpu.SMEM)
    f32, bf16, dma = jnp.float32, jnp.bfloat16, pltpu.SemaphoreType.DMA
    precond, scale = pl.pallas_call(
        functools.partial(fused_kernel, group_count, shard_count, tok_rows, main, group_count * width * ff_full),
        out_shape=(
            pltpu.VMEM((width, ff_dev), f32),
            jax.ShapeDtypeStruct((8, 128), f32),
        ),
        in_specs=[smem, smem, vmem, vmem, vmem],
        out_specs=(vmem, vmem),
        scratch_shapes=[
            pltpu.VMEM((total, main, ff_dev + BLK), bf16),
            pltpu.VMEM((group_count, tall, MARK), bf16),
            pltpu.VMEM((4, total, tok_rows, width // 4), bf16),
            pltpu.VMEM((total, main, ff_dev + BLK), bf16),
            pltpu.VMEM((total, tall, MARK), bf16),
            pltpu.VMEM((row_total, BLK), bf16),
            pltpu.VMEM((row_total, width), bf16),
            pltpu.VMEM((row_total, ff_dev), bf16),
            pltpu.VMEM((count_a + blocks, BLK, BLK), f32),
            pltpu.VMEM((count * LEAF // 128, LEAF, 128), f32),
            pltpu.VMEM((count * LEAF // 128, LEAF, 128), f32),
            pltpu.VMEM((count * LEAF // 128, LEAF, 128), f32),
            pltpu.VMEM((count, HALF, HALF), f32),
            pltpu.VMEM((count, HALF, HALF), f32),
            pltpu.VMEM((count, HALF // 2, HALF // 2), f32),
            pltpu.VMEM((8, BLK), f32),
            pltpu.VMEM((total, 8, MARK), f32),
            dma((8 * depth,)),
            dma((8 * depth,)),
            dma((8 * depth,)),
            dma((16 * depth,)),
            dma((total,)),
            dma((4 * total,)),
            dma((total,)),
            dma((6,)),
            dma((total,)),
            dma((total,)),
            dma((total,)),
            dma((total,)),
        ],
        compiler_params=pltpu.CompilerParams(collective_id=0, has_side_effects=True, vmem_limit_bytes=36 << 20),
    )(
        d_levels[0],
        f_levels[0],
        tokens_in,
        out_grad.reshape(2 * tok_rows, ff_full),
        expert_ids.reshape(1, 2 * tok_rows),
    )
    ascent = pl.pallas_call(
        scale_kernel,
        out_shape=jax.ShapeDtypeStruct((width, ff_dev), bf16),
        in_specs=[vmem, vmem],
        out_specs=pl.BlockSpec(memory_space=pl.ANY),
        scratch_shapes=[pltpu.VMEM((4, BLK, ff_dev), bf16), dma((4,))],
        compiler_params=pltpu.CompilerParams(vmem_limit_bytes=8 << 20),
    )(precond, scale)
    return ascent[None]


def local(tokens_in, out_grad, expert_ids, d_levels, f_levels):
    group_count = lax.axis_size("expert")
    shard_count = lax.axis_size("shard")
    tok_rows, width = tokens_in.shape
    blocks = out_grad.shape[2] // shard_count // BLK
    main = 16 * (capacity_of(tok_rows, group_count) // 16)
    extra = capacity_of(tok_rows, group_count) - main
    chips = group_count // 2 == 2 and shard_count % 2 == 0
    packed = main > 0 and extra * blocks == main and MARK % tok_rows == 0 and (main + extra) % (MARK // tok_rows) == 0
    even = (group_count * shard_count * tok_rows) % BLK == 0 and width % (8 * BLK) == 0 and blocks % 4 == 0
    small = group_count * shard_count * tok_rows * width * 2 <= 12 << 20
    if chips and packed and even and small:
        return fast(tokens_in, out_grad, expert_ids, d_levels, f_levels)
    return plain(tokens_in, out_grad, expert_ids, d_levels, f_levels)


def solution(mesh):
    return jax.shard_map(
        local,
        mesh=mesh,
        in_specs=(
            P(("expert", "shard"), None),
            P(("expert", "shard"), None, None),
            P(("expert", "shard"), None),
            P("expert", None),
            P("expert", "shard"),
        ),
        out_specs=P("expert", None, "shard"),
        check_vma=False,
    )
```
